256 devices in a mesh: ctx: 32 (over y, z), tp: 8 (over x, core).
Axes of the slice: x: 4, y: 4, z: 8, core: 2. Of those that a mesh axis runs over, the one named last changes fastest.
Arguments:
- values_in: bfloat16 [8192, 8192], P('ctx', 'tp'), may hold values from -6 to 6
- gate_in: bfloat16 [8192, 8192], P('ctx', 'tp'), may hold values from -6 to 6
- keys_in: bfloat16 [8192, 1024], P('ctx', 'tp'), may hold values from -3 to 3
- queries_in: bfloat16 [8192, 1024], P('ctx', 'tp'), may hold values from -3 to 3
- step_in: bfloat16 [8192, 128], P('ctx', 'tp'), may hold values from -4 to 4
- block_order: int32 [128], replicated, may hold values from 0 to 127, as said below
- doc_lengths: int32 [16], replicated, may hold values from 1 to 4096, 8192 in all
- conv_values: float32 [4, 8192], P(None, 'tp'), may hold values from -3 to 3
- conv_keys: float32 [4, 1024], P(None, 'tp'), may hold values from -3 to 3
- conv_queries: float32 [4, 1024], P(None, 'tp'), may hold values from -3 to 3
- decay_log: float32 [128], P('tp'), may hold values from -7 to 0, as said below
- step_bias: float32 [128], P('tp'), may hold values from -9 to -2, as said below
- skip_gain: float32 [128], P('tp'), may hold values from 0.5 to 2
- norm_gain: float32 [8192], P('tp'), may hold values from 0.25 to 1.75
- out_weight: bfloat16 [8192, 4096], P('tp'), may hold values from -0.0625 to 0.0625
Outputs:
- layer_out: bfloat16 [8192, 4096], P(('ctx', 'tp'))
The draws below stay inside these ranges and needn't reach their ends.
Inputs may be any that keep to these rules, and one draw needn't show every extreme that they name: `block_order`: loaded block j sits on loader j // 4; sequence block q belongs to owner q // 4; every block appears once; the 4 blocks of each loader belong to 4 different owners. `doc_lengths`: document lengths in sequence order; they sum to 8192 and the longest is exactly 4096. `decay_log`: logarithm of each head's decay coefficient. `step_bias`: bias added to each head's time-step pre-activation.
All inputs are finite; a program needn't handle non-finite values.
Results may differ from the reference program's by a relative error of at most 0.02.
Values may be sent and summed in bfloat16 or wider, within the bound.
A program may use at most 128 MiB of HBM per device.

```python
import math
import jax
import jax.numpy as jnp
import numpy as np
from jax import lax

HEADS = 128
HEAD_DIM = 64
STATE = 128
GROUPS = 8
CONV = 4
OUTW = 4096
SPAN = 256
BLK = 64
DOCS = 16
TOKENS = 8192
NBLK = 128
BLK_DEV = 4
CAP = 1
N_CTX = 32
N_TP = 8


def draw_block_order(key, part):
    loaders = N_CTX
    per_dev = BLK_DEV
    capacity = CAP
    subkeys = jax.random.split(jax.random.fold_in(key, 3), 5)
    spare = jax.random.permutation(subkeys[0], (loaders - 1) * capacity).astype(jnp.int32)
    distances = jnp.concatenate([jnp.zeros((capacity,), jnp.int32), 1 + spare[:per_dev - capacity] % (loaders - 1)])
    loader_ids = jnp.arange(loaders, dtype=jnp.int32)
    owner_linear = (loader_ids[:, None] + distances[None, :]) % loaders
    loader_shuffle = jax.random.permutation(subkeys[1], loaders).astype(jnp.int32)
    owner_shuffle = jax.random.permutation(subkeys[2], loaders).astype(jnp.int32)
    owners = owner_shuffle[owner_linear].reshape(-1)
    scores = jax.random.permutation(subkeys[3], loaders * per_dev).astype(jnp.int32)
    ranked_ahead = (owners[None, :] == owners[:, None]) & (scores[None, :] < scores[:, None])
    slot_rank = jnp.sum(ranked_ahead.astype(jnp.int32), axis=1, dtype=jnp.int32)
    sequence_block = (owners * per_dev + slot_rank).reshape(loaders, per_dev)
    shuffle_scores = jax.random.permutation(subkeys[4], loaders * per_dev).astype(jnp.int32).reshape(loaders, per_dev)
    local_order = jnp.argsort(shuffle_scores, axis=1, stable=True)
    arranged = jnp.take_along_axis(sequence_block, local_order, axis=1)
    placed = jnp.zeros((loaders, per_dev), jnp.int32).at[loader_shuffle].set(arranged)
    return placed.reshape(-1)


def head_table(key):
    base = jax.random.fold_in(key, 11)
    pick_key, fast_key, slow_key, jitter_key = jax.random.split(base, 4)
    fast_heads = jax.random.randint(pick_key, (HEADS,), 0, 8) < 4
    fast_log = jax.random.uniform(fast_key, (HEADS,), jnp.float32, math.log(30.0), math.log(50.0))
    slow_log = jax.random.uniform(slow_key, (HEADS,), jnp.float32, math.log(TOKENS / 2.0), math.log(TOKENS * 4.0))
    memory_log = jnp.where(fast_heads, fast_log, slow_log)
    jitter = jax.random.uniform(jitter_key, (HEADS,), jnp.float32, -0.7, 0.7)
    step_log = math.log(0.5) - 0.5 * memory_log + jitter
    return (memory_log, step_log)


def draw_decay_log(key, part):
    memory_log, step_log = head_table(key)
    return (-memory_log - step_log).astype(jnp.float32)


def draw_step_bias(key, part):
    memory_log, step_log = head_table(key)
    return (step_log - 0.5).astype(jnp.float32)


def block_scale(own_key, shape, cuts, low, top_value):
    def one(dim, blocks):
        draws = jax.random.uniform(jax.random.fold_in(jax.random.fold_in(own_key, 6), dim), (blocks,), jnp.float32, low / len(cuts), top_value / len(cuts))
        return jnp.repeat(jnp.exp(draws), shape[dim] // blocks).reshape((-1,) + (1,) * (len(shape) - dim - 1))

    level = one(*cuts[0])
    for cut in cuts[1:]:
        level = level * one(*cut)
    return level


def profile(number_of, total, reach, lean):
    loads = [(1 << 20) // math.isqrt(rank ** lean) + 1 for rank in range(2, number_of + 1)]
    surplus, given = total - reach - (number_of - 1), [1] * (number_of - 1)
    while surplus > 0:
        movable = [i for i in range(number_of - 1) if given[i] < reach]
        pool, budget = sum([loads[i] for i in movable]), surplus
        for i in movable:
            addition = min(reach - given[i], max(1, budget * loads[i] // pool), surplus)
            given[i] = given[i] + addition
            surplus = surplus - addition
    return np.array([reach] + given)


def ragged(rng, number_of, total, limit, lean):
    if number_of == 2:
        one = jax.random.randint(rng, (), max(1, total - limit), min(limit, total - 1) + 1)
        return jnp.stack([one, total - one])
    tallies = jnp.asarray(profile(number_of, total, limit, lean), jnp.int32)
    twos = (number_of - 1) // 2
    giver, receiver = tallies[1:1 + 2 * twos:2], tallies[2:2 + 2 * twos:2]
    slack = jnp.minimum(giver - 1, limit - receiver)
    passed = jax.random.randint(jax.random.fold_in(rng, 1), (twos,), 0, 1 << 20) % (slack + 1)
    tallies = tallies.at[1:1 + 2 * twos:2].set(giver - passed).at[2:2 + 2 * twos:2].set(receiver + passed)
    return tallies[jax.random.permutation(jax.random.fold_in(rng, 2), number_of)]


def noise(rng, dims, deviation, limit, cuts=(), kind=jnp.bfloat16):
    entries = jax.random.normal(rng, dims, jnp.float32) * deviation
    if len(cuts) > 0:
        entries = block_scale(rng, dims, cuts, -0.22, 0.18) * entries
    return jnp.clip(entries, min=-limit, max=limit).astype(kind)


def setup_inputs(seed: int = 0) -> dict:
    splits = jax.random.split(jax.random.key(seed), 16)
    values_in = noise(splits[0], (TOKENS, HEADS * HEAD_DIM), 1.0, 6.0, ((0, 32), (1, 8)))
    gate_in = noise(splits[1], (TOKENS, HEADS * HEAD_DIM), 1.0, 6.0, ((0, 32), (1, 8)))
    keys_in = noise(splits[2], (TOKENS, GROUPS * STATE), 0.5, 3.0, ((0, 32), (1, 8)))
    queries_in = noise(splits[3], (TOKENS, GROUPS * STATE), 0.5, 3.0, ((0, 32), (1, 8)))
    step_in = noise(splits[4], (TOKENS, HEADS), 1.0, 4.0, ((0, 32), (1, 8)))
    block_order = draw_block_order(jax.random.fold_in(splits[15], 71), 0)
    doc_lengths = ragged(splits[6], DOCS, TOKENS, TOKENS // 2, 2).astype(jnp.int32)
    conv_values = noise(splits[7], (CONV, HEADS * HEAD_DIM), 0.5, 3.0, ((1, 8),), jnp.float32)
    conv_keys = noise(splits[8], (CONV, GROUPS * STATE), 0.5, 3.0, ((1, 8),), jnp.float32)
    conv_queries = noise(splits[9], (CONV, GROUPS * STATE), 0.5, 3.0, ((1, 8),), jnp.float32)
    decay_log = draw_decay_log(jax.random.fold_in(splits[15], 71), 0)
    step_bias = draw_step_bias(jax.random.fold_in(splits[15], 71), 0)
    skip_gain = jnp.clip(jnp.exp(math.log(2.0) - 1.3862944 * jax.random.uniform(splits[12], (HEADS,), jnp.float32) ** block_scale(splits[12], (HEADS,), ((0, 8),), -0.2, 0.2)), 0.5, 2.0)
    norm_gain = jnp.clip(1.0 + 0.15 * jax.random.normal(splits[13], (HEADS * HEAD_DIM,), jnp.float32), 0.25, 1.75)
    out_weight = noise(splits[14], (HEADS * HEAD_DIM, OUTW), (HEADS * HEAD_DIM) ** -0.5, 0.0625, ((0, 8),))
    return {"values_in": values_in, "gate_in": gate_in, "keys_in": keys_in, "queries_in": queries_in, "step_in": step_in, "block_order": block_order, "doc_lengths": doc_lengths, "conv_values": conv_values, "conv_keys": conv_keys, "conv_queries": conv_queries, "decay_log": decay_log, "step_bias": step_bias, "skip_gain": skip_gain, "norm_gain": norm_gain, "out_weight": out_weight}


def document_index(positions, doc_lengths):
    offsets = jnp.cumsum(doc_lengths) - doc_lengths
    below_start = offsets[None, :] <= positions[:, None]
    documents = lax.optimization_barrier(jnp.sum(below_start.astype(jnp.int32), axis=1, dtype=jnp.int32)) - 1
    openings = jnp.any(offsets[None, :] == positions[:, None], axis=1).astype(jnp.int32)
    return (documents, openings)

def causal_conv(extended, weight, doc_ext):
    tap_count = weight.shape[0]
    row_count = extended.shape[0] - tap_count + 1
    current = doc_ext[tap_count - 1:]
    accumulated = jnp.zeros((row_count, extended.shape[1]), jnp.float32)
    for tap_index in range(tap_count):
        keep_rows = (doc_ext[tap_index:tap_index + row_count] == current)[:, None]
        shifted = extended[tap_index:tap_index + row_count].astype(jnp.float32) * weight[tap_index]
        accumulated = accumulated + jnp.where(keep_rows, shifted, 0.0)
    return lax.optimization_barrier(jax.nn.silu(accumulated).astype(jnp.bfloat16))

def span_outputs(value_rows, step_rows, key_rows, query_rows, decay_sums, documents):
    row_count = value_rows.shape[0]
    per_group = value_rows.shape[1] // key_rows.shape[1]
    row_ids = jnp.arange(row_count, dtype=jnp.int32)
    keep_mask = (documents[:, None] == documents[None, :]) & (row_ids[None, :] <= row_ids[:, None])
    differences = decay_sums[:, :, None] - decay_sums[:, None, :]
    decays = jnp.where(keep_mask[None], jnp.exp(jnp.minimum(differences, 0.0)), 0.0)
    inner_products = jnp.einsum('ign,jgn->gij', query_rows.astype(jnp.float32), key_rows.astype(jnp.float32), precision=lax.Precision.HIGHEST)
    weighted = (decays * jnp.repeat(inner_products, per_group, axis=0) * step_rows.T[:, None, :]).astype(jnp.bfloat16)
    return jnp.einsum('hij,jhp->ihp', weighted.astype(jnp.float32), value_rows.astype(jnp.float32), precision=lax.Precision.HIGHEST)

def span_states(value_rows, step_rows, key_rows, decay_sums, documents, openings):
    per_group = value_rows.shape[1] // key_rows.shape[1]
    tail_decay = jnp.where((documents == documents[-1])[None, :], jnp.exp(decay_sums[:, -1:] - decay_sums), 0.0)
    tail_weight = tail_decay.T * step_rows
    head_keys = jnp.repeat(key_rows.astype(jnp.float32), per_group, axis=1)
    tail_keys = (tail_weight[:, :, None] * head_keys).astype(jnp.bfloat16)
    local_state = jnp.einsum('jhp,jhn->hpn', value_rows.astype(jnp.float32), tail_keys.astype(jnp.float32), precision=lax.Precision.HIGHEST)
    opened = jnp.cumsum(openings)
    span_gate = jnp.where(opened[-1] == 0, jnp.exp(decay_sums[:, -1]), 0.0)
    inflow = jnp.where((opened == 0)[None, :], jnp.exp(decay_sums), 0.0)
    return (local_state, span_gate, inflow)

def span_inflow(query_rows, entering, inflow):
    per_group = entering.shape[0] // query_rows.shape[1]
    head_queries = jnp.repeat(query_rows.astype(jnp.float32), per_group, axis=1)
    carried = jnp.einsum('ihn,hpn->ihp', head_queries, entering, precision=lax.Precision.HIGHEST)
    return carried * inflow.T[:, :, None]

def gated_norm(mixed_rows, gate_rows, norm_gain, groups_local):
    gated_rows = mixed_rows * jax.nn.silu(gate_rows.astype(jnp.float32))
    grouped = gated_rows.reshape(gated_rows.shape[0], groups_local, -1)
    inverse_rms = lax.rsqrt(lax.optimization_barrier(jnp.mean(grouped * grouped, axis=2, keepdims=True)) + 1e-05)
    return ((grouped * inverse_rms).reshape(gated_rows.shape) * norm_gain).astype(jnp.bfloat16)

def reference(values_in, gate_in, keys_in, queries_in, step_in, block_order, doc_lengths, conv_values, conv_keys, conv_queries, decay_log, step_bias, skip_gain, norm_gain, out_weight):

    def to_sequence(loaded):
        blocks = loaded.reshape(NBLK, BLK, loaded.shape[1])
        placed = jnp.zeros_like(blocks).at[block_order].set(blocks)
        return placed.reshape(TOKENS, loaded.shape[1])
    value_seq = to_sequence(values_in)
    gate_seq = to_sequence(gate_in)
    key_seq = to_sequence(keys_in)
    query_seq = to_sequence(queries_in)
    step_seq = to_sequence(step_in)
    rim_rows = CONV - 1
    positions = jnp.arange(TOKENS + rim_rows, dtype=jnp.int32) - rim_rows
    doc_ext, open_ext = document_index(positions, doc_lengths)
    documents = doc_ext[rim_rows:]
    openings = open_ext[rim_rows:]
    width_local = HEADS * HEAD_DIM // N_TP
    state_local = GROUPS * STATE // N_TP
    heads_local = HEADS // N_TP
    groups_local = GROUPS // N_TP
    span_count = TOKENS // SPAN

    def padded(rows):
        return jnp.concatenate([jnp.zeros((rim_rows, rows.shape[1]), rows.dtype), rows], axis=0)

    def advance(carried, inputs):
        value_rows, key_rows, query_rows, step_rows, rate_rows, span_docs, span_openings = inputs
        decay_sums = jnp.cumsum(rate_rows.T, axis=1)
        intra = span_outputs(value_rows, step_rows, key_rows, query_rows, decay_sums, span_docs)
        local_state, span_gate, inflow = span_states(value_rows, step_rows, key_rows, decay_sums, span_docs, span_openings)
        inter = span_inflow(query_rows, carried, inflow)
        return (span_gate[:, None, None] * carried + local_state, intra + inter)
    accumulated = jnp.zeros((TOKENS, OUTW), jnp.float32)
    for group_index in range(N_TP):
        channel_lo = group_index * width_local
        state_lo = group_index * state_local
        head_lo = group_index * heads_local
        conv_value = causal_conv(padded(value_seq[:, channel_lo:channel_lo + width_local]), conv_values[:, channel_lo:channel_lo + width_local], doc_ext)
        conv_key = causal_conv(padded(key_seq[:, state_lo:state_lo + state_local]), conv_keys[:, state_lo:state_lo + state_local], doc_ext)
        conv_query = causal_conv(padded(query_seq[:, state_lo:state_lo + state_local]), conv_queries[:, state_lo:state_lo + state_local], doc_ext)
        step_size = jax.nn.softplus(step_seq[:, head_lo:head_lo + heads_local].astype(jnp.float32) + step_bias[head_lo:head_lo + heads_local])
        rates = -jnp.exp(decay_log[head_lo:head_lo + heads_local]) * step_size
        value_rows = conv_value.reshape(span_count, SPAN, heads_local, HEAD_DIM)
        key_rows = conv_key.reshape(span_count, SPAN, groups_local, STATE)
        query_rows = conv_query.reshape(span_count, SPAN, groups_local, STATE)
        start_state = jnp.zeros((heads_local, HEAD_DIM, STATE), jnp.float32)
        inputs = (value_rows, key_rows, query_rows, step_size.reshape(span_count, SPAN, heads_local), rates.reshape(span_count, SPAN, heads_local), documents.reshape(span_count, SPAN), openings.reshape(span_count, SPAN))
        final_state, outputs = lax.scan(advance, start_state, inputs)
        mixed_rows = outputs + skip_gain[head_lo:head_lo + heads_local][None, None, :, None] * value_rows.astype(jnp.float32)
        mixed_rows = mixed_rows.reshape(TOKENS, width_local)
        normed = gated_norm(mixed_rows, gate_seq[:, channel_lo:channel_lo + width_local], norm_gain[channel_lo:channel_lo + width_local], groups_local)
        partial_value = jnp.dot(normed, out_weight[channel_lo:channel_lo + width_local], preferred_element_type=jnp.float32).astype(jnp.bfloat16)
        partial_value = lax.optimization_barrier(partial_value)
        accumulated = accumulated + partial_value.astype(jnp.float32)
    return accumulated.astype(jnp.bfloat16)
```

```python
import functools

import jax
import jax.numpy as jnp
from jax import lax
from jax.experimental import pallas as pl
from jax.experimental.pallas import tpu as pltpu
from jax.sharding import PartitionSpec as P

NC = 32
BPD = 4
BLK = 64
SPAN = 256
WIDTH = 1024
HEADS = 16
STATE = 128
OUTW = 4096
DOCS = 16
NCHUNK = 8
CW = OUTW // NCHUNK
MESH = pl.DeviceIdType.MESH
F32 = jnp.float32
BF16 = jnp.bfloat16
HIGHEST = lax.Precision.HIGHEST


def silu(x):
    return x * jax.nn.sigmoid(x)


def iota(shape, axis):
    return lax.broadcasted_iota(jnp.int32, shape, axis)


def body(
    inv,
    doc_lengths,
    skip,
    values,
    gates,
    keys,
    queries,
    steps,
    taps_v,
    taps_k,
    taps_q,
    decay_log,
    step_bias,
    norm_gain,
    weight_hbm,
    out,
    weight,
    step_pad,
    rows16,
    recv_v,
    recv_g,
    recv_s,
    send_v,
    send_g,
    send_s,
    main_v,
    main_g,
    main_s,
    rim_v,
    rim_s,
    conv_v,
    conv_k,
    conv_q,
    masks,
    product,
    tail_x,
    inflow_x,
    st_send,
    st_recv,
    ent_send,
    ent,
    y,
    normed,
    s1_send,
    s1_recv,
    own_part,
    s2_send,
    s2_recv,
    w_sem,
    v_send,
    v_recv,
    g_send,
    g_recv,
    k_send,
    k_recv,
    v2_send,
    v2_recv,
    g2_send,
    g2_recv,
    k2_send,
    k2_recv,
    rv_send,
    rv_recv,
    rk_send,
    rk_recv,
    st_ss,
    st_rs,
    en_ss,
    en_rs,
    s1_ss,
    s1_rs,
    s2_ss,
    s2_rs,
):
    me = lax.axis_index("ctx")
    tp = lax.axis_index("tp")
    my_x = lax.div(tp, 2)
    core = lax.rem(tp, 2)
    sibling = my_x * 2 + (1 - core)

    weight_copy = pltpu.make_async_copy(weight_hbm, weight, w_sem)
    weight_copy.start()

    barrier = pltpu.get_barrier_semaphore()

    def peer(d):
        return lax.rem(me + d, NC)

    def greet(d, carry):
        pl.semaphore_signal(barrier, inc=1, device_id={"ctx": peer(d)}, device_id_type=MESH)
        return carry

    lax.fori_loop(1, NC, greet, 0)
    pl.semaphore_signal(barrier, inc=1, device_id={"tp": sibling}, device_id_type=MESH)
    for dx in range(1, 4):
        other = lax.rem(my_x + dx, 4) * 2 + core
        pl.semaphore_signal(barrier, inc=1, device_id={"tp": other}, device_id_type=MESH)

    step_pad[...] = jnp.zeros_like(step_pad)
    step_pad[:, :, 0:HEADS] = steps[...]
    rows16[...] = jnp.zeros_like(rows16)
    rows16[0:1, 0:HEADS] = step_bias[...]
    rows16[1:2, 0:HEADS] = decay_log[...]

    pl.semaphore_wait(barrier, NC - 1 + 4)

    def remote(src, dst, ss, rs, where):
        return pltpu.make_async_remote_copy(
            src_ref=src, dst_ref=dst, send_sem=ss, recv_sem=rs, device_id=where, device_id_type=MESH
        )

    def piece(ref, c):
        return ref.at[:, pl.ds(pl.multiple_of(16 * lax.rem(c, 4), 16), 16), pl.ds(pl.multiple_of(128 * lax.div(c, 4), 128), 128)]

    def octet(ref, c):
        return ref.at[:, pl.ds(pl.multiple_of(8 * lax.rem(c, 8), 8), 8), :]

    my_slots = pl.ds(BPD * me, BPD)

    def small_source(c, act):
        @pl.when(c < 8)
        def _():
            act(octet(keys, c))

        @pl.when((c >= 8) & (c < 16))
        def _():
            act(octet(queries, c))

        @pl.when((c >= 16) & (c < 24))
        def _():
            act(octet(step_pad, c))

    def first_v(d, carry):
        c = peer(d)
        where = {"ctx": c}
        small_source(c, lambda src: remote(src, recv_s.at[my_slots], k_send, k_recv, where).start())
        remote(piece(values, c), recv_v.at[my_slots], v_send, v_recv, where).start()
        return carry

    small_source(me, lambda src: pltpu.make_async_copy(src, recv_s.at[my_slots], k_recv).start())
    pltpu.make_async_copy(piece(values, me), recv_v.at[my_slots], v_recv).start()
    lax.fori_loop(1, NC, first_v, 0)

    def first_g(d, carry):
        c = peer(d)
        remote(piece(gates, c), recv_g.at[my_slots], g_send, g_recv, {"ctx": c}).start()
        return carry

    pltpu.make_async_copy(piece(gates, me), recv_g.at[my_slots], g_recv).start()
    lax.fori_loop(1, NC, first_g, 0)

    starts = []
    total = jnp.int32(0)
    for k in range(DOCS):
        starts.append(total - me * SPAN)
        total = total + doc_lengths[k]

    row = iota((SPAN, 128), 0)

    def opening_at(position):
        hit = position == starts[0]
        for k in range(1, DOCS):
            hit = hit | (position == starts[k])
        return hit

    open0 = opening_at(row)
    open1 = opening_at(row - 1)
    open2 = opening_at(row - 2)
    masks[0] = jnp.where(open0 | open1 | open2, 0.0, 1.0).astype(F32)
    masks[1] = jnp.where(open0 | open1, 0.0, 1.0).astype(F32)
    masks[2] = jnp.where(open0, 0.0, 1.0).astype(F32)

    later = starts[0] < -SPAN
    tail_cut = jnp.zeros((SPAN, 128), jnp.int32)
    head_cut = jnp.zeros((SPAN, 128), jnp.int32)
    for k in range(DOCS):
        inside = (row * 0 + starts[k] >= 0) & (row * 0 + starts[k] < SPAN)
        tail_cut = tail_cut | jnp.where(inside & (row < starts[k]), 1, 0)
        head_cut = head_cut | jnp.where(inside & (row >= starts[k]), 1, 0)
    del later

    def permute(src, dst):
        def one(q, carry):
            dst[q] = src[inv[q]]
            return carry

        lax.fori_loop(0, NC * BPD, one, 0, unroll=8)

    def owner_slots(o):
        return pl.ds(BPD * o, BPD)

    def before(o):
        return lax.rem(BPD * o + NC * BPD - 1, NC * BPD)

    has_small = me < 24
    kind = lax.div(me, 8)

    def small_target(i, o):
        return main_s.at[i, :, pl.ds(pl.multiple_of(8 * lax.rem(me, 8), 8), 8), :]

    @pl.when(has_small)
    def _():
        pltpu.make_async_copy(recv_s, recv_s, k_recv).wait()
        permute(recv_s, send_s)
        sends_rim = (lax.rem(me, 8) == 7) & (me < 16)

        def second_s(d, carry):
            o = peer(d)
            where = {"ctx": o}
            remote(send_s.at[owner_slots(o)], small_target(kind, o), k2_send, k2_recv, where).start()

            @pl.when(sends_rim)
            def _():
                remote(send_s.at[before(o)], rim_s.at[kind], rk_send, rk_recv, where).start()

            return carry

        pltpu.make_async_copy(send_s.at[owner_slots(me)], small_target(kind, me), k2_recv).start()

        @pl.when(sends_rim)
        def _():
            pltpu.make_async_copy(send_s.at[before(me)], rim_s.at[kind], rk_recv).start()

        lax.fori_loop(1, NC, second_s, 0)

    pltpu.make_async_copy(recv_v, recv_v, v_recv).wait()
    permute(recv_v, send_v)
    v_rim = lax.rem(me, 4) == 3

    def rim_target():
        return rim_v.at[:, pl.ds(pl.multiple_of(128 * lax.div(me, 4), 128), 128)]

    def second_v(d, carry):
        o = peer(d)
        where = {"ctx": o}
        remote(send_v.at[owner_slots(o)], piece(main_v, me), v2_send, v2_recv, where).start()

        @pl.when(v_rim)
        def _():
            remote(send_v.at[before(o)], rim_target(), rv_send, rv_recv, where).start()

        return carry

    pltpu.make_async_copy(send_v.at[owner_slots(me)], piece(main_v, me), v2_recv).start()

    @pl.when(v_rim)
    def _():
        pltpu.make_async_copy(send_v.at[before(me)], rim_target(), rv_recv).start()

    lax.fori_loop(1, NC, second_v, 0)

    pltpu.make_async_copy(main_s, main_s, k2_recv).wait()
    pltpu.make_async_copy(rim_s, rim_s, rk_recv).wait()

    def conv(rim, rows, taps):
        ext = jnp.concatenate([rim, rows], axis=0)
        acc = (masks[0] * taps[0:1, :]) * pltpu.roll(ext, 3, 0)[8:, :]
        acc = acc + (masks[1] * taps[1:2, :]) * pltpu.roll(ext, 2, 0)[8:, :]
        acc = acc + (masks[2] * taps[2:3, :]) * pltpu.roll(ext, 1, 0)[8:, :]
        acc = acc + taps[3:4, :] * rows
        return silu(acc)

    key_f = conv(rim_s[0].astype(F32), main_s[0].reshape(SPAN, 128).astype(F32), taps_k)
    query_f = conv(rim_s[1].astype(F32), main_s[1].reshape(SPAN, 128).astype(F32), taps_q)
    conv_k[...] = key_f.astype(BF16)
    conv_q[...] = query_f.astype(BF16)

    pre = main_s[2].reshape(SPAN, 128).astype(F32) + rows16[0:1, :]
    small = jnp.exp(-jnp.abs(pre))
    one_more = 1.0 + small
    gap = one_more - 1.0
    log1p = jnp.where(gap == 0.0, small, jnp.log(one_more) * small / jnp.where(gap == 0.0, 1.0, gap))
    step = jnp.maximum(pre, 0.0) + log1p
    sums = -jnp.exp(rows16[1:2, :]) * step
    for k in (1, 2, 4, 8, 16, 32, 64, 128):
        sums = sums + jnp.where(row >= k, pltpu.roll(sums, k, 0), 0.0)
    last = sums[SPAN - 1 : SPAN, :]
    tail = jnp.where(tail_cut > 0, 0.0, jnp.exp(last - sums) * step)
    inflow = jnp.where(head_cut > 0, 0.0, jnp.exp(sums))
    spread = jnp.where(
        lax.div(iota((128, WIDTH), 1), 64) == iota((128, WIDTH), 0), 1.0, 0.0
    ).astype(F32)
    tail_x[...] = jnp.dot(tail, spread, precision=HIGHEST, preferred_element_type=F32)
    inflow_x[...] = jnp.dot(inflow, spread, precision=HIGHEST, preferred_element_type=F32)
    gate_row = inflow_x[SPAN - 1 : SPAN, :]
    gate_hi = gate_row.astype(BF16)
    gate_lo = (gate_row - gate_hi.astype(F32)).astype(BF16)
    which = iota((8, WIDTH), 0)
    gate_rows = jnp.where(
        which == 0, gate_hi.astype(F32), jnp.where(which == 1, gate_lo.astype(F32), 0.0)
    ).astype(BF16)
    sums_t = jnp.transpose(sums)
    step_t = jnp.transpose(step)
    key_t = jnp.transpose(conv_k[...].astype(F32)).astype(BF16)
    t_id = iota((SPAN, SPAN), 0)
    u_id = iota((SPAN, SPAN), 1)
    drop = u_id > t_id
    for k in range(DOCS):
        drop = drop | ((u_id < starts[k]) & (t_id >= starts[k]))
    inner = lax.dot_general(
        conv_q[...], conv_k[...], (((1,), (1,)), ((), ())), preferred_element_type=F32
    )
    product[...] = jnp.where(drop, 0.0, inner)

    pltpu.make_async_copy(main_v, main_v, v2_recv).wait()
    pltpu.make_async_copy(rim_v, rim_v, rv_recv).wait()
    for g in range(8):
        lanes = slice(128 * g, 128 * g + 128)
        rows = main_v[:, :, lanes].reshape(SPAN, 128).astype(F32)
        rim = rim_v[:, lanes].astype(F32)[8:16, :]
        conv_v[:, lanes] = conv(rim, rows, taps_v[:, lanes]).astype(BF16)

    scaled = (conv_v[...].astype(F32) * tail_x[...]).astype(BF16)
    local = jnp.dot(key_t, scaled, preferred_element_type=F32).astype(BF16)
    for r in range(4):
        st_send[r, 0:32, :] = local[32 * r : 32 * r + 32, :]
        st_send[r, 32:40, :] = gate_rows

    def state_piece(c):
        return st_send.at[lax.rem(c, 4), :, pl.ds(pl.multiple_of(128 * lax.div(c, 4), 128), 128)]

    def send_state(d, carry):
        c = peer(d)
        remote(state_piece(c), st_recv.at[me], st_ss, st_rs, {"ctx": c}).start()
        return carry

    pltpu.make_async_copy(state_piece(me), st_recv.at[me], st_rs).start()
    lax.fori_loop(1, NC, send_state, 0)

    pltpu.make_async_copy(recv_g, recv_g, g_recv).wait()
    permute(recv_g, send_g)

    def second_g(d, carry):
        o = peer(d)
        remote(send_g.at[owner_slots(o)], piece(main_g, me), g2_send, g2_recv, {"ctx": o}).start()
        return carry

    pltpu.make_async_copy(send_g.at[owner_slots(me)], piece(main_g, me), g2_recv).start()
    lax.fori_loop(1, NC, second_g, 0)

    left = iota((SPAN, 128), 1) < 64

    def intra(g):
        lanes = slice(128 * g, 128 * g + 128)
        pair = conv_v[:, lanes]
        found = []
        for h in (2 * g, 2 * g + 1):
            decay = jnp.exp(jnp.minimum(sums[:, h : h + 1] - sums_t[h : h + 1, :], 0.0))
            mix = (decay * (product[...] * step_t[h : h + 1, :])).astype(BF16)
            found.append(jnp.dot(mix, pair, preferred_element_type=F32))
        gain = jnp.where(left, skip[2 * g], skip[2 * g + 1])
        y[:, lanes] = jnp.where(left, found[0], found[1]) + gain * pair.astype(F32)

    for g in range(4):
        intra(g)

    pltpu.make_async_copy(st_recv, st_recv, st_rs).wait()
    state = jnp.zeros((32, 128), F32)
    for o in range(NC):
        ent_send[o] = state.astype(BF16)
        part = st_recv[o, 0:32, :].astype(F32)
        pair = st_recv[o, 32:40, :].astype(F32)
        state = (pair[0:1, :] + pair[1:2, :]) * state + part

    def ent_target():
        return ent.at[pl.ds(pl.multiple_of(32 * lax.rem(me, 4), 32), 32), pl.ds(pl.multiple_of(128 * lax.div(me, 4), 128), 128)]

    def send_ent(d, carry):
        o = peer(d)
        remote(ent_send.at[o], ent_target(), en_ss, en_rs, {"ctx": o}).start()
        return carry

    pltpu.make_async_copy(ent_send.at[me], ent_target(), en_rs).start()
    lax.fori_loop(1, NC, send_ent, 0)

    for g in range(4, 8):
        intra(g)

    pltpu.make_async_copy(ent, ent, en_rs).wait()
    pltpu.make_async_copy(main_g, main_g, g2_recv).wait()
    squares = jnp.zeros((SPAN, 128), F32)
    for g in range(8):
        lanes = slice(128 * g, 128 * g + 128)
        carried = jnp.dot(conv_q[...], ent[:, lanes], preferred_element_type=F32)
        gate = main_g[:, :, lanes].reshape(SPAN, 128).astype(F32)
        gated = (y[:, lanes] + inflow_x[:, lanes] * carried) * silu(gate)
        squares = squares + gated * gated
        y[:, lanes] = gated
    mean = jnp.sum(squares, axis=1, keepdims=True) * (1.0 / WIDTH)
    scale = lax.rsqrt(mean + 1e-05)
    normed[...] = (y[...] * scale * norm_gain[...]).astype(BF16)

    weight_copy.wait()

    def s1_copy(i):
        return remote(s1_send.at[i], s1_recv.at[i], s1_ss.at[i], s1_rs.at[i], {"tp": sibling})

    def s2_copy(i, dx):
        xx = lax.rem(my_x + dx, 4)
        return remote(
            s2_send.at[i, dx - 1],
            s2_recv.at[i, 3 - dx],
            s2_ss.at[i, dx - 1],
            s2_rs.at[i, 3 - dx],
            {"tp": xx * 2 + core},
        )

    def project(i):
        cols = pl.ds(pl.multiple_of(CW * i, CW), CW)
        part = jnp.dot(normed[...], weight[:, cols], preferred_element_type=F32)
        own_part[...] = part.reshape(4, 2, 32, CW)
        s1_send[i] = own_part[:, 1 - core].astype(BF16)
        s1_copy(i).start()
        keep = own_part[:, core]
        return keep

    def finish(i, keep_ref):
        s1_copy(i).wait_recv()
        keep_ref[i] = keep_ref[i] + s1_recv[i].astype(F32)
        for dx in range(1, 4):
            xx = lax.rem(my_x + dx, 4)
            s2_send[i, dx - 1] = keep_ref[i, xx].astype(BF16)
            s2_copy(i, dx).start()

    def run(keep_ref):
        for i in range(NCHUNK + 1):
            if i < NCHUNK:
                keep_ref[i] = project(i)
            if i > 0:
                finish(i - 1, keep_ref)
        for i in range(NCHUNK):
            for dx in range(1, 4):
                s2_copy(i, dx).wait_recv()
            both = keep_ref[i, my_x]
            for k in range(3):
                both = both + s2_recv[i, k].astype(F32)
            out[:, CW * i : CW * i + CW] = both.astype(BF16)

    pl.run_scoped(run, pltpu.VMEM((NCHUNK, 4, 32, CW), F32))

    most = pl.ds(0, BPD * (NC - 1))
    for ref, sem in ((recv_v, v_send), (recv_g, g_send), (send_v, v2_send), (send_g, g2_send)):
        pltpu.make_async_copy(ref.at[most], ref.at[most], sem).wait()

    @pl.when(me < 24)
    def _():
        some = recv_s.at[pl.ds(0, BPD * 23)]
        pltpu.make_async_copy(some, some, k_send).wait()
        some = send_s.at[most]
        pltpu.make_async_copy(some, some, k2_send).wait()

    @pl.when(me >= 24)
    def _():
        some = recv_s.at[pl.ds(0, BPD * 24)]
        pltpu.make_async_copy(some, some, k_send).wait()

    @pl.when(v_rim)
    def _():
        some = send_v.at[pl.ds(0, NC - 1)]
        pltpu.make_async_copy(some, some, rv_send).wait()

    @pl.when((lax.rem(me, 8) == 7) & (me < 16))
    def _():
        some = send_s.at[pl.ds(0, NC - 1)]
        pltpu.make_async_copy(some, some, rk_send).wait()

    some = st_recv.at[pl.ds(0, NC - 1)]
    pltpu.make_async_copy(some, some, st_ss).wait()
    some = ent_send.at[pl.ds(0, NC - 1)]
    pltpu.make_async_copy(some, some, en_ss).wait()
    for i in range(NCHUNK):
        s1_copy(i).wait_send()
        for dx in range(1, 4):
            s2_copy(i, dx).wait_send()


def on_device(
    values_in,
    gate_in,
    keys_in,
    queries_in,
    step_in,
    block_order,
    doc_lengths,
    conv_values,
    conv_keys,
    conv_queries,
    decay_log,
    step_bias,
    skip_gain,
    norm_gain,
    out_weight,
):
    count = NC * BPD
    ids = jnp.arange(count, dtype=jnp.int32)
    inverse = jnp.sum(
        jnp.where(block_order[None, :] == ids[:, None], ids[None, :], 0), axis=1, dtype=jnp.int32
    )
    vmem = pl.BlockSpec(memory_space=pltpu.VMEM)
    smem = pl.BlockSpec(memory_space=pltpu.SMEM)
    hbm = pl.BlockSpec(memory_space=pl.ANY)
    dma = pltpu.SemaphoreType.DMA
    scratch = [
        pltpu.VMEM((WIDTH, OUTW), BF16),
        pltpu.VMEM((BPD, BLK, 128), BF16),
        pltpu.VMEM((8, 128), F32),
        pltpu.VMEM((count, 16, 128), BF16),
        pltpu.VMEM((count, 16, 128), BF16),
        pltpu.VMEM((count, 8, 128), BF16),
        pltpu.VMEM((count, 16, 128), BF16),
        pltpu.VMEM((count, 16, 128), BF16),
        pltpu.VMEM((count, 8, 128), BF16),
        pltpu.VMEM((BPD, BLK, WIDTH), BF16),
        pltpu.VMEM((BPD, BLK, WIDTH), BF16),
        pltpu.VMEM((3, BPD, BLK, 128), BF16),
        pltpu.VMEM((16, WIDTH), BF16),
        pltpu.VMEM((2, 8, 128), BF16),
        pltpu.VMEM((SPAN, WIDTH), BF16),
        pltpu.VMEM((SPAN, STATE), BF16),
        pltpu.VMEM((SPAN, STATE), BF16),
        pltpu.VMEM((3, SPAN, 128), F32),
        pltpu.VMEM((SPAN, SPAN), F32),
        pltpu.VMEM((SPAN, WIDTH), F32),
        pltpu.VMEM((SPAN, WIDTH), F32),
        pltpu.VMEM((4, 40, WIDTH), BF16),
        pltpu.VMEM((NC, 40, 128), BF16),
        pltpu.VMEM((NC, 32, 128), BF16),
        pltpu.VMEM((STATE, WIDTH), BF16),
        pltpu.VMEM((SPAN, WIDTH), F32),
        pltpu.VMEM((SPAN, WIDTH), BF16),
        pltpu.VMEM((NCHUNK, 4, 32, CW), BF16),
        pltpu.VMEM((NCHUNK, 4, 32, CW), BF16),
        pltpu.VMEM((4, 2, 32, CW), F32),
        pltpu.VMEM((NCHUNK, 3, 32, CW), BF16),
        pltpu.VMEM((NCHUNK, 3, 32, CW), BF16),
        dma(()),
    ]
    scratch += [dma(()) for _ in range(16)]
    scratch += [dma(()) for _ in range(4)]
    scratch += [dma((NCHUNK,)), dma((NCHUNK,)), dma((NCHUNK, 3)), dma((NCHUNK, 3))]
    call = pl.pallas_call(
        body,
        out_shape=jax.ShapeDtypeStruct((SPAN // 8, OUTW), BF16),
        in_specs=[smem, smem, smem, hbm, hbm, hbm, hbm, vmem, vmem, vmem, vmem, vmem, vmem, vmem, hbm],
        out_specs=vmem,
        scratch_shapes=scratch,
        compiler_params=pltpu.CompilerParams(
            collective_id=0, has_side_effects=True, vmem_limit_bytes=48 << 20
        ),
        name="layer",
    )
    return call(
        inverse,
        doc_lengths,
        skip_gain,
        values_in.reshape(BPD, BLK, WIDTH),
        gate_in.reshape(BPD, BLK, WIDTH),
        keys_in.reshape(BPD, BLK, STATE),
        queries_in.reshape(BPD, BLK, STATE),
        step_in.reshape(BPD, BLK, HEADS),
        conv_values,
        conv_keys,
        conv_queries,
        decay_log.reshape(1, HEADS),
        step_bias.reshape(1, HEADS),
        norm_gain.reshape(1, WIDTH),
        out_weight,
    )


def solution(mesh):
    in_specs = (
        P("ctx", "tp"),
        P("ctx", "tp"),
        P("ctx", "tp"),
        P("ctx", "tp"),
        P("ctx", "tp"),
        P(),
        P(),
        P(None, "tp"),
        P(None, "tp"),
        P(None, "tp"),
        P("tp"),
        P("tp"),
        P("tp"),
        P("tp"),
        P("tp", None),
    )
    out_specs = P(("ctx", "tp"), None)
    return jax.shard_map(
        on_device, mesh=mesh, in_specs=in_specs, out_specs=out_specs, check_vma=False
    )
```

```python
import functools

import jax
import jax.numpy as jnp
from jax import lax
from jax.experimental import pallas as pl
from jax.experimental.pallas import tpu as pltpu
from jax.sharding import PartitionSpec as P

NC = 32
BPD = 4
BLK = 64
SPAN = 256
WIDTH = 1024
HEADS = 16
STATE = 128
OUTW = 4096
DOCS = 16
NCHUNK = 8
CW = OUTW // NCHUNK
FIRST_G = 12
SECOND_G = 16
MESH = pl.DeviceIdType.MESH
F32 = jnp.float32
BF16 = jnp.bfloat16
HIGHEST = lax.Precision.HIGHEST


def silu(x):
    return x * jax.nn.sigmoid(x)


def iota(shape, axis):
    return lax.broadcasted_iota(jnp.int32, shape, axis)


def body(
    order_hbm,
    lengths_hbm,
    skip_hbm,
    values,
    gates,
    keys,
    queries,
    steps_hbm,
    taps_v_hbm,
    taps_k_hbm,
    taps_q_hbm,
    decay_hbm,
    bias_hbm,
    gain_hbm,
    weight_hbm,
    out,
    order,
    doc_lengths,
    skip,
    steps_in,
    taps_v,
    taps_k,
    taps_q,
    decay_log,
    step_bias,
    norm_gain,
    inv_row,
    inv,
    local_sem,
    inv_sem,
    weight,
    step_pad,
    rows16,
    recv_v,
    recv_g,
    recv_s,
    send_v,
    send_g,
    send_s,
    main_v,
    main_g,
    main_s,
    rim_v,
    rim_s,
    rim_send_v,
    rim_send_s,
    conv_v,
    conv_k,
    conv_q,
    masks,
    product,
    tail_x,
    inflow_x,
    st_send,
    st_recv,
    ent_send,
    ent,
    y,
    normed,
    s1_send,
    s1_recv,
    own_part,
    keep,
    far_send,
    far_recv,
    near_send,
    near_recv,
    last_send,
    last_recv,
    w_sem,
    v_send,
    v_recv,
    g_send,
    g_recv,
    k_send,
    k_recv,
    v2_send,
    v2_recv,
    g2_send,
    g2_recv,
    k2_send,
    k2_recv,
    rv_send,
    rv_recv,
    rk_send,
    rk_recv,
    st_ss,
    st_rs,
    en_ss,
    en_rs,
    s1_ss,
    s1_rs,
    s2_ss,
    s2_rs,
):
    me = lax.axis_index("ctx")
    tp = lax.axis_index("tp")
    my_x = lax.div(tp, 2)
    core = lax.rem(tp, 2)
    sibling = my_x * 2 + (1 - core)

    loads = [
        pltpu.make_async_copy(src, dst, local_sem.at[i])
        for i, (src, dst) in enumerate(
            (
                (steps_hbm, steps_in),
                (order_hbm, order),
                (lengths_hbm, doc_lengths),
                (skip_hbm, skip),
                (taps_v_hbm, taps_v),
                (taps_k_hbm, taps_k),
                (taps_q_hbm, taps_q),
                (decay_hbm, decay_log),
                (bias_hbm, step_bias),
                (gain_hbm, norm_gain),
            )
        )
    ]
    barrier = pltpu.get_barrier_semaphore()

    def peer(d):
        return lax.rem(me + d, NC)

    def greet(d, carry):
        pl.semaphore_signal(barrier, inc=1, device_id={"ctx": peer(d)}, device_id_type=MESH)
        return carry

    lax.fori_loop(1, NC, greet, 0)
    pl.semaphore_signal(barrier, inc=1, device_id={"tp": sibling}, device_id_type=MESH)
    for dx in (1, 3):
        other = lax.rem(my_x + dx, 4) * 2 + core
        pl.semaphore_signal(barrier, inc=1, device_id={"tp": other}, device_id_type=MESH)

    for load in loads:
        load.start()
    pl.semaphore_wait(barrier, NC - 1 + 3)

    def remote(src, dst, ss, rs, where):
        return pltpu.make_async_remote_copy(
            src_ref=src, dst_ref=dst, send_sem=ss, recv_sem=rs, device_id=where, device_id_type=MESH
        )

    def piece(ref, c):
        return ref.at[:, pl.ds(pl.multiple_of(16 * lax.rem(c, 4), 16), 16), pl.ds(pl.multiple_of(128 * lax.div(c, 4), 128), 128)]

    def octet(ref, c):
        return ref.at[:, pl.ds(pl.multiple_of(8 * lax.rem(c, 8), 8), 8), :]

    my_slots = pl.ds(BPD * me, BPD)

    def small_source(c, act):
        @pl.when(c < 8)
        def _():
            act(octet(keys, c))

        @pl.when((c >= 8) & (c < 16))
        def _():
            act(octet(queries, c))

    def step_source(c, act):
        @pl.when((c >= 16) & (c < 24))
        def _():
            act(octet(step_pad, c))

    def first_v(d, carry):
        c = peer(d)
        where = {"ctx": c}
        small_source(c, lambda src: remote(src, recv_s.at[my_slots], k_send, k_recv, where).start())
        remote(piece(values, c), recv_v.at[my_slots], v_send, v_recv, where).start()
        return carry

    lax.fori_loop(1, NC, first_v, 0)
    small_source(me, lambda src: pltpu.make_async_copy(src, recv_s.at[my_slots], k_recv).start())
    pltpu.make_async_copy(piece(values, me), recv_v.at[my_slots], v_recv).start()

    for load in loads:
        load.wait()
    wide = jnp.concatenate(
        [steps_in[...].astype(F32), jnp.zeros((128 - HEADS, SPAN), F32)], axis=0
    )
    step_pad[...] = jnp.transpose(wide).astype(BF16).reshape(BPD, BLK, 128)
    rows16[...] = jnp.zeros_like(rows16)
    rows16[0:1, 0:HEADS] = step_bias[...]
    rows16[1:2, 0:HEADS] = decay_log[...]
    side = (NC * BPD, NC * BPD)
    placed = jnp.transpose(jnp.broadcast_to(order[...], side))
    found_at = jnp.where(placed == iota(side, 1), iota(side, 0), 0)
    inv_row[0:1, :] = jnp.max(found_at, axis=0, keepdims=True)
    inv_copy = pltpu.make_async_copy(inv_row, inv, inv_sem)
    inv_copy.start()

    def first_step(c, carry):
        @pl.when(c != me)
        def _():
            remote(octet(step_pad, c), recv_s.at[my_slots], k_send, k_recv, {"ctx": c}).start()

        return carry

    lax.fori_loop(16, 24, first_step, 0)
    step_source(me, lambda src: pltpu.make_async_copy(src, recv_s.at[my_slots], k_recv).start())

    def first_g(d, carry):
        c = peer(d)
        remote(piece(gates, c), recv_g.at[my_slots], g_send, g_recv, {"ctx": c}).start()
        return carry

    lax.fori_loop(1, FIRST_G, first_g, 0)
    weight_copy = pltpu.make_async_copy(weight_hbm, weight, w_sem)
    weight_copy.start()
    inv_copy.wait()

    starts = []
    total = jnp.int32(0)
    for k in range(DOCS):
        starts.append(total - me * SPAN)
        total = total + doc_lengths[0, k]

    row = iota((SPAN, 128), 0)

    def opening_at(position):
        hit = position == starts[0]
        for k in range(1, DOCS):
            hit = hit | (position == starts[k])
        return hit

    open0 = opening_at(row)
    open1 = opening_at(row - 1)
    open2 = opening_at(row - 2)
    masks[0] = jnp.where(open0 | open1 | open2, 0.0, 1.0).astype(F32)
    masks[1] = jnp.where(open0 | open1, 0.0, 1.0).astype(F32)
    masks[2] = jnp.where(open0, 0.0, 1.0).astype(F32)

    tail_cut = jnp.zeros((SPAN, 128), jnp.int32)
    head_cut = jnp.zeros((SPAN, 128), jnp.int32)
    for k in range(DOCS):
        inside = (row * 0 + starts[k] >= 0) & (row * 0 + starts[k] < SPAN)
        tail_cut = tail_cut | jnp.where(inside & (row < starts[k]), 1, 0)
        head_cut = head_cut | jnp.where(inside & (row >= starts[k]), 1, 0)

    def owner_slots(o):
        return pl.ds(BPD * o, BPD)

    def fill(src, dst, o):
        for k in range(BPD):
            dst[BPD * o + k] = src[inv[0, BPD * o + k]]

    def before(o):
        return inv[0, lax.rem(BPD * o + NC * BPD - 1, NC * BPD)]

    has_small = me < 24
    kind = lax.div(me, 8)

    def small_target(i):
        return main_s.at[i, :, pl.ds(pl.multiple_of(8 * lax.rem(me, 8), 8), 8), :]

    @pl.when(has_small)
    def _():
        pltpu.make_async_copy(recv_s, recv_s, k_recv).wait()
        sends_rim = (lax.rem(me, 8) == 7) & (me < 16)

        def second_s(d, carry):
            o = peer(d)
            where = {"ctx": o}
            fill(recv_s, send_s, o)
            remote(send_s.at[owner_slots(o)], small_target(kind), k2_send, k2_recv, where).start()

            @pl.when(sends_rim)
            def _():
                rim_send_s[o] = recv_s[before(o)]
                remote(rim_send_s.at[o], rim_s.at[kind], rk_send, rk_recv, where).start()

            return carry

        lax.fori_loop(1, NC, second_s, 0)
        fill(recv_s, send_s, me)
        pltpu.make_async_copy(send_s.at[owner_slots(me)], small_target(kind), k2_recv).start()

        @pl.when(sends_rim)
        def _():
            rim_send_s[me] = recv_s[before(me)]
            pltpu.make_async_copy(rim_send_s.at[me], rim_s.at[kind], rk_recv).start()

    pltpu.make_async_copy(recv_v, recv_v, v_recv).wait()
    v_rim = lax.rem(me, 4) == 3

    def rim_target():
        return rim_v.at[:, pl.ds(pl.multiple_of(128 * lax.div(me, 4), 128), 128)]

    def second_v(d, carry):
        o = peer(d)
        where = {"ctx": o}
        fill(recv_v, send_v, o)
        remote(send_v.at[owner_slots(o)], piece(main_v, me), v2_send, v2_recv, where).start()

        @pl.when(v_rim)
        def _():
            rim_send_v[o] = recv_v[before(o)]
            remote(rim_send_v.at[o], rim_target(), rv_send, rv_recv, where).start()

        return carry

    lax.fori_loop(1, NC, second_v, 0)
    fill(recv_v, send_v, me)
    pltpu.make_async_copy(send_v.at[owner_slots(me)], piece(main_v, me), v2_recv).start()

    @pl.when(v_rim)
    def _():
        rim_send_v[me] = recv_v[before(me)]
        pltpu.make_async_copy(rim_send_v.at[me], rim_target(), rv_recv).start()

    lax.fori_loop(FIRST_G, NC, first_g, 0)
    pltpu.make_async_copy(piece(gates, me), recv_g.at[my_slots], g_recv).start()

    pltpu.make_async_copy(main_s, main_s, k2_recv).wait()
    pltpu.make_async_copy(rim_s, rim_s, rk_recv).wait()

    def conv(rim, rows, taps):
        ext = jnp.concatenate([rim, rows], axis=0)
        acc = (masks[0] * taps[0:1, :]) * pltpu.roll(ext, 3, 0)[8:, :]
        acc = acc + (masks[1] * taps[1:2, :]) * pltpu.roll(ext, 2, 0)[8:, :]
        acc = acc + (masks[2] * taps[2:3, :]) * pltpu.roll(ext, 1, 0)[8:, :]
        acc = acc + taps[3:4, :] * rows
        return silu(acc)

    key_f = conv(rim_s[0].astype(F32), main_s[0].reshape(SPAN, 128).astype(F32), taps_k)
    query_f = conv(rim_s[1].astype(F32), main_s[1].reshape(SPAN, 128).astype(F32), taps_q)
    conv_k[...] = key_f.astype(BF16)
    conv_q[...] = query_f.astype(BF16)

    pre = main_s[2].reshape(SPAN, 128).astype(F32) + rows16[0:1, :]
    small = jnp.exp(-jnp.abs(pre))
    one_more = 1.0 + small
    gap = one_more - 1.0
    log1p = jnp.where(gap == 0.0, small, jnp.log(one_more) * small / jnp.where(gap == 0.0, 1.0, gap))
    step = jnp.maximum(pre, 0.0) + log1p
    sums = -jnp.exp(rows16[1:2, :]) * step
    for k in (1, 2, 4, 8, 16, 32, 64, 128):
        sums = sums + jnp.where(row >= k, pltpu.roll(sums, k, 0), 0.0)
    last = sums[SPAN - 1 : SPAN, :]
    tail = jnp.where(tail_cut > 0, 0.0, jnp.exp(last - sums) * step)
    inflow = jnp.where(head_cut > 0, 0.0, jnp.exp(sums))
    spread = jnp.where(
        lax.div(iota((128, WIDTH), 1), 64) == iota((128, WIDTH), 0), 1.0, 0.0
    ).astype(F32)
    tail_x[...] = jnp.dot(tail, spread, precision=HIGHEST, preferred_element_type=F32)
    inflow_x[...] = jnp.dot(inflow, spread, precision=HIGHEST, preferred_element_type=F32)
    gate_row = inflow_x[SPAN - 1 : SPAN, :]
    gate_hi = gate_row.astype(BF16)
    gate_lo = (gate_row - gate_hi.astype(F32)).astype(BF16)
    which = iota((8, WIDTH), 0)
    gate_rows = jnp.where(
        which == 0, gate_hi.astype(F32), jnp.where(which == 1, gate_lo.astype(F32), 0.0)
    ).astype(BF16)
    sums_t = jnp.transpose(sums)
    step_t = jnp.transpose(step)
    key_t = jnp.transpose(conv_k[...].astype(F32)).astype(BF16)
    t_id = iota((SPAN, SPAN), 0)
    u_id = iota((SPAN, SPAN), 1)
    drop = u_id > t_id
    for k in range(DOCS):
        drop = drop | ((u_id < starts[k]) & (t_id >= starts[k]))
    inner = lax.dot_general(
        conv_q[...], conv_k[...], (((1,), (1,)), ((), ())), preferred_element_type=F32
    )
    product[...] = jnp.where(drop, 0.0, inner)

    pltpu.make_async_copy(main_v, main_v, v2_recv).wait()
    pltpu.make_async_copy(rim_v, rim_v, rv_recv).wait()
    for g in range(8):
        lanes = slice(128 * g, 128 * g + 128)
        rows = main_v[:, :, lanes].reshape(SPAN, 128).astype(F32)
        rim = rim_v[:, lanes].astype(F32)[8:16, :]
        conv_v[:, lanes] = conv(rim, rows, taps_v[:, lanes]).astype(BF16)

    scaled = (conv_v[...].astype(F32) * tail_x[...]).astype(BF16)
    local = jnp.dot(key_t, scaled, preferred_element_type=F32).astype(BF16)
    for r in range(4):
        st_send[r, 0:32, :] = local[32 * r : 32 * r + 32, :]
        st_send[r, 32:40, :] = gate_rows

    def state_piece(c):
        return st_send.at[lax.rem(c, 4), :, pl.ds(pl.multiple_of(128 * lax.div(c, 4), 128), 128)]

    def send_state(d, carry):
        c = peer(d)
        remote(state_piece(c), st_recv.at[me], st_ss, st_rs, {"ctx": c}).start()
        return carry

    pltpu.make_async_copy(state_piece(me), st_recv.at[me], st_rs).start()
    lax.fori_loop(1, NC, send_state, 0)

    def second_g(d, carry):
        o = peer(d)
        fill(recv_g, send_g, o)
        remote(send_g.at[owner_slots(o)], piece(main_g, me), g2_send, g2_recv, {"ctx": o}).start()
        return carry

    left = iota((SPAN, 128), 1) < 64

    def intra(g):
        lanes = slice(128 * g, 128 * g + 128)
        pair = conv_v[:, lanes]
        found = []
        for h in (2 * g, 2 * g + 1):
            decay = jnp.exp(jnp.minimum(sums[:, h : h + 1] - sums_t[h : h + 1, :], 0.0))
            mix = (decay * (product[...] * step_t[h : h + 1, :])).astype(BF16)
            found.append(jnp.dot(mix, pair, preferred_element_type=F32))
        gain = jnp.where(left, skip[0, 2 * g], skip[0, 2 * g + 1])
        y[:, lanes] = jnp.where(left, found[0], found[1]) + gain * pair.astype(F32)

    for g in range(3):
        intra(g)

    pltpu.make_async_copy(recv_g, recv_g, g_recv).wait()
    lax.fori_loop(1, SECOND_G, second_g, 0)

    for g in range(3, 6):
        intra(g)

    pltpu.make_async_copy(st_recv, st_recv, st_rs).wait()
    state = jnp.zeros((32, 128), F32)
    for o in range(NC):
        ent_send[o] = state.astype(BF16)
        part = st_recv[o, 0:32, :].astype(F32)
        pair = st_recv[o, 32:40, :].astype(F32)
        state = (pair[0:1, :] + pair[1:2, :]) * state + part

    def ent_target():
        return ent.at[pl.ds(pl.multiple_of(32 * lax.rem(me, 4), 32), 32), pl.ds(pl.multiple_of(128 * lax.div(me, 4), 128), 128)]

    def send_ent(d, carry):
        o = peer(d)
        remote(ent_send.at[o], ent_target(), en_ss, en_rs, {"ctx": o}).start()
        return carry

    pltpu.make_async_copy(ent_send.at[me], ent_target(), en_rs).start()
    lax.fori_loop(1, NC, send_ent, 0)

    lax.fori_loop(SECOND_G, NC, second_g, 0)
    fill(recv_g, send_g, me)
    pltpu.make_async_copy(send_g.at[owner_slots(me)], piece(main_g, me), g2_recv).start()

    for g in range(6, 8):
        intra(g)

    pltpu.make_async_copy(ent, ent, en_rs).wait()
    for g in range(8):
        lanes = slice(128 * g, 128 * g + 128)
        carried = jnp.dot(conv_q[...], ent[:, lanes], preferred_element_type=F32)
        y[:, lanes] = y[:, lanes] + inflow_x[:, lanes] * carried

    pltpu.make_async_copy(main_g, main_g, g2_recv).wait()
    squares = jnp.zeros((SPAN, 128), F32)
    for g in range(8):
        lanes = slice(128 * g, 128 * g + 128)
        gate = main_g[:, :, lanes].reshape(SPAN, 128).astype(F32)
        gated = y[:, lanes] * silu(gate)
        squares = squares + gated * gated
        y[:, lanes] = gated
    mean = jnp.sum(squares, axis=1, keepdims=True) * (1.0 / WIDTH)
    scale = lax.rsqrt(mean + 1e-05)
    normed[...] = (y[...] * scale * norm_gain[...]).astype(BF16)

    weight_copy.wait()

    def s1_copy(i):
        return remote(s1_send.at[i], s1_recv.at[i], s1_ss.at[i], s1_rs.at[i], {"tp": sibling})

    def turn(i):
        return 1 if i % 2 == 0 else 3

    def along(i, step):
        return {"tp": lax.rem(my_x + step, 4) * 2 + core}

    def far_copy(i):
        return remote(far_send.at[i], far_recv.at[i], s2_ss.at[i, 0], s2_rs.at[i, 0], along(i, turn(i)))

    def near_copy(i):
        return remote(
            near_send.at[i], near_recv.at[i], s2_ss.at[i, 1], s2_rs.at[i, 1], along(i, 4 - turn(i))
        )

    def last_copy(i):
        return remote(last_send.at[i], last_recv.at[i], s2_ss.at[i, 2], s2_rs.at[i, 2], along(i, turn(i)))

    for i in range(NCHUNK + 2):
        if i < NCHUNK:
            part = jnp.dot(normed[...], weight[:, CW * i : CW * i + CW], preferred_element_type=F32)
            own_part[...] = part.reshape(4, 2, 32, CW)
            s1_send[i] = own_part[:, 1 - core].astype(BF16)
            s1_copy(i).start()
            keep[i] = own_part[:, core]
        if 1 <= i <= NCHUNK:
            k = i - 1
            s1_copy(k).wait_recv()
            keep[k] = keep[k] + s1_recv[k].astype(F32)
            far_send[k] = keep[k, lax.rem(my_x + 2, 4)].astype(BF16)
            far_copy(k).start()
            near_send[k] = keep[k, lax.rem(my_x + 4 - turn(k), 4)].astype(BF16)
            near_copy(k).start()
        if i >= 2:
            k = i - 2
            far_copy(k).wait_recv()
            both = keep[k, lax.rem(my_x + turn(k), 4)] + far_recv[k].astype(F32)
            last_send[k] = both.astype(BF16)
            last_copy(k).start()

    for i in range(NCHUNK):
        near_copy(i).wait_recv()
        last_copy(i).wait_recv()
        both = keep[i, my_x] + near_recv[i].astype(F32) + last_recv[i].astype(F32)
        out[:, CW * i : CW * i + CW] = both.astype(BF16)

    most = pl.ds(0, BPD * (NC - 1))
    for ref, sem in ((recv_v, v_send), (recv_g, g_send), (send_v, v2_send), (send_g, g2_send)):
        pltpu.make_async_copy(ref.at[most], ref.at[most], sem).wait()

    @pl.when(me < 24)
    def _():
        some = recv_s.at[pl.ds(0, BPD * 23)]
        pltpu.make_async_copy(some, some, k_send).wait()
        some = send_s.at[most]
        pltpu.make_async_copy(some, some, k2_send).wait()

    @pl.when(me >= 24)
    def _():
        some = recv_s.at[pl.ds(0, BPD * 24)]
        pltpu.make_async_copy(some, some, k_send).wait()

    @pl.when(v_rim)
    def _():
        some = rim_send_v.at[pl.ds(0, NC - 1)]
        pltpu.make_async_copy(some, some, rv_send).wait()

    @pl.when((lax.rem(me, 8) == 7) & (me < 16))
    def _():
        some = rim_send_s.at[pl.ds(0, NC - 1)]
        pltpu.make_async_copy(some, some, rk_send).wait()

    some = st_recv.at[pl.ds(0, NC - 1)]
    pltpu.make_async_copy(some, some, st_ss).wait()
    some = ent_send.at[pl.ds(0, NC - 1)]
    pltpu.make_async_copy(some, some, en_ss).wait()
    for i in range(NCHUNK):
        s1_copy(i).wait_send()
        far_copy(i).wait_send()
        near_copy(i).wait_send()
        last_copy(i).wait_send()


def on_device(
    values_in,
    gate_in,
    keys_in,
    queries_in,
    step_in,
    block_order,
    doc_lengths,
    conv_values,
    conv_keys,
    conv_queries,
    decay_log,
    step_bias,
    skip_gain,
    norm_gain,
    out_weight,
):
    count = NC * BPD
    vmem = pl.BlockSpec(memory_space=pltpu.VMEM)
    hbm = pl.BlockSpec(memory_space=pltpu.HBM)
    dma = pltpu.SemaphoreType.DMA
    scratch = [
        pltpu.VMEM((1, count), jnp.int32),
        pltpu.SMEM((1, DOCS), jnp.int32),
        pltpu.SMEM((1, HEADS), F32),
        pltpu.VMEM((HEADS, SPAN), BF16),
        pltpu.VMEM((4, WIDTH), F32),
        pltpu.VMEM((4, STATE), F32),
        pltpu.VMEM((4, STATE), F32),
        pltpu.VMEM((1, HEADS), F32),
        pltpu.VMEM((1, HEADS), F32),
        pltpu.VMEM((1, WIDTH), F32),
        pltpu.VMEM((1, count), jnp.int32),
        pltpu.SMEM((1, count), jnp.int32),
        dma((10,)),
        dma(()),
        pltpu.VMEM((WIDTH, OUTW), BF16),
        pltpu.VMEM((BPD, BLK, 128), BF16),
        pltpu.VMEM((8, 128), F32),
        pltpu.VMEM((count, 16, 128), BF16),
        pltpu.VMEM((count, 16, 128), BF16),
        pltpu.VMEM((count, 8, 128), BF16),
        pltpu.VMEM((count, 16, 128), BF16),
        pltpu.VMEM((count, 16, 128), BF16),
        pltpu.VMEM((count, 8, 128), BF16),
        pltpu.VMEM((BPD, BLK, WIDTH), BF16),
        pltpu.VMEM((BPD, BLK, WIDTH), BF16),
        pltpu.VMEM((3, BPD, BLK, 128), BF16),
        pltpu.VMEM((16, WIDTH), BF16),
        pltpu.VMEM((2, 8, 128), BF16),
        pltpu.VMEM((NC, 16, 128), BF16),
        pltpu.VMEM((NC, 8, 128), BF16),
        pltpu.VMEM((SPAN, WIDTH), BF16),
        pltpu.VMEM((SPAN, STATE), BF16),
        pltpu.VMEM((SPAN, STATE), BF16),
        pltpu.VMEM((3, SPAN, 128), F32),
        pltpu.VMEM((SPAN, SPAN), F32),
        pltpu.VMEM((SPAN, WIDTH), F32),
        pltpu.VMEM((SPAN, WIDTH), F32),
        pltpu.VMEM((4, 40, WIDTH), BF16),
        pltpu.VMEM((NC, 40, 128), BF16),
        pltpu.VMEM((NC, 32, 128), BF16),
        pltpu.VMEM((STATE, WIDTH), BF16),
        pltpu.VMEM((SPAN, WIDTH), F32),
        pltpu.VMEM((SPAN, WIDTH), BF16),
        pltpu.VMEM((NCHUNK, 4, 32, CW), BF16),
        pltpu.VMEM((NCHUNK, 4, 32, CW), BF16),
        pltpu.VMEM((4, 2, 32, CW), F32),
        pltpu.VMEM((NCHUNK, 4, 32, CW), F32),
        pltpu.VMEM((NCHUNK, 32, CW), BF16),
        pltpu.VMEM((NCHUNK, 32, CW), BF16),
        pltpu.VMEM((NCHUNK, 32, CW), BF16),
        pltpu.VMEM((NCHUNK, 32, CW), BF16),
        pltpu.VMEM((NCHUNK, 32, CW), BF16),
        pltpu.VMEM((NCHUNK, 32, CW), BF16),
        dma(()),
    ]
    scratch += [dma(()) for _ in range(16)]
    scratch += [dma(()) for _ in range(4)]
    scratch += [dma((NCHUNK,)), dma((NCHUNK,)), dma((NCHUNK, 3)), dma((NCHUNK, 3))]
    call = pl.pallas_call(
        body,
        out_shape=jax.ShapeDtypeStruct((SPAN // 8, OUTW), BF16),
        in_specs=[hbm] * 15,
        out_specs=vmem,
        scratch_shapes=scratch,
        compiler_params=pltpu.CompilerParams(
            collective_id=0, has_side_effects=True, vmem_limit_bytes=60 << 20
        ),
        name="layer",
    )
    return call(
        block_order.reshape(1, count),
        doc_lengths.reshape(1, DOCS),
        skip_gain.reshape(1, HEADS),
        values_in.reshape(BPD, BLK, WIDTH),
        gate_in.reshape(BPD, BLK, WIDTH),
        keys_in.reshape(BPD, BLK, STATE),
        queries_in.reshape(BPD, BLK, STATE),
        step_in.T,
        conv_values,
        conv_keys,
        conv_queries,
        decay_log.reshape(1, HEADS),
        step_bias.reshape(1, HEADS),
        norm_gain.reshape(1, WIDTH),
        out_weight,
    )


def solution(mesh):
    in_specs = (
        P("ctx", "tp"),
        P("ctx", "tp"),
        P("ctx", "tp"),
        P("ctx", "tp"),
        P("ctx", "tp"),
        P(),
        P(),
        P(None, "tp"),
        P(None, "tp"),
        P(None, "tp"),
        P("tp"),
        P("tp"),
        P("tp"),
        P("tp"),
        P("tp", None),
    )
    out_specs = P(("ctx", "tp"), None)
    return jax.shard_map(
        on_device, mesh=mesh, in_specs=in_specs, out_specs=out_specs, check_vma=False
    )
```

```python
import functools

import jax
import jax.numpy as jnp
from jax import lax
from jax.experimental import pallas as pl
from jax.experimental.pallas import tpu as pltpu
from jax.sharding import PartitionSpec as P

NC = 32
BPD = 4
BLK = 64
SPAN = 256
WIDTH = 1024
HEADS = 16
STATE = 128
OUTW = 4096
DOCS = 16
NCHUNK = 8
CW = OUTW // NCHUNK
FIRST_G = 12
MESH = pl.DeviceIdType.MESH
F32 = jnp.float32
BF16 = jnp.bfloat16
HIGHEST = lax.Precision.HIGHEST


def silu(x):
    return x * jax.nn.sigmoid(x)


def iota(shape, axis):
    return lax.broadcasted_iota(jnp.int32, shape, axis)


def body(
    order_hbm,
    lengths_hbm,
    skip_hbm,
    values,
    gates,
    keys,
    queries,
    steps_hbm,
    taps_v_hbm,
    taps_k_hbm,
    taps_q_hbm,
    decay_hbm,
    bias_hbm,
    gain_hbm,
    weight_hbm,
    out,
    order,
    doc_lengths,
    skip,
    steps_in,
    taps_v,
    taps_k,
    taps_q,
    decay_log,
    step_bias,
    norm_gain,
    inv_row,
    inv,
    local_sem,
    inv_sem,
    weight,
    step_pad,
    rows16,
    recv_v,
    recv_g,
    recv_s,
    send_v,
    send_g,
    send_s,
    main_v,
    main_g,
    main_s,
    rim_v,
    rim_s,
    rim_send_v,
    rim_send_s,
    conv_v,
    conv_k,
    conv_q,
    masks,
    product,
    tail_x,
    inflow_x,
    st_send,
    st_recv,
    ent_send,
    ent,
    y,
    normed,
    s1_send,
    s1_recv,
    own_part,
    keep,
    pair_send,
    pair_recv,
    last_send,
    last_recv,
    w_sem,
    v_send,
    v_recv,
    g_send,
    g_recv,
    k_send,
    k_recv,
    v2_send,
    v2_recv,
    g2_send,
    g2_recv,
    k2_send,
    k2_recv,
    rv_send,
    rv_recv,
    rk_send,
    rk_recv,
    st_ss,
    st_rs,
    en_ss,
    en_rs,
    s1_ss,
    s1_rs,
    p_ss,
    p_rs,
    l_ss,
    l_rs,
):
    me = lax.axis_index("ctx")
    tp = lax.axis_index("tp")
    my_x = lax.div(tp, 2)
    core = lax.rem(tp, 2)
    sibling = my_x * 2 + (1 - core)

    loads = [
        pltpu.make_async_copy(src, dst, local_sem.at[i])
        for i, (src, dst) in enumerate(
            (
                (steps_hbm, steps_in),
                (order_hbm, order),
                (lengths_hbm, doc_lengths),
                (skip_hbm, skip),
                (taps_v_hbm, taps_v),
                (taps_k_hbm, taps_k),
                (taps_q_hbm, taps_q),
                (decay_hbm, decay_log),
                (bias_hbm, step_bias),
                (gain_hbm, norm_gain),
            )
        )
    ]
    barrier = pltpu.get_barrier_semaphore()

    def peer(d):
        return lax.rem(me + d, NC)

    def greet(d, carry):
        pl.semaphore_signal(barrier, inc=1, device_id={"ctx": peer(d)}, device_id_type=MESH)
        return carry

    lax.fori_loop(1, NC, greet, 0)
    pl.semaphore_signal(barrier, inc=1, device_id={"tp": sibling}, device_id_type=MESH)
    parity = lax.rem(my_x, 2)
    partner = (my_x + 1 - 2 * parity) * 2 + core
    across = (3 - my_x) * 2 + core
    for other in (partner, across):
        pl.semaphore_signal(barrier, inc=1, device_id={"tp": other}, device_id_type=MESH)

    for load in loads:
        load.start()
    pl.semaphore_wait(barrier, NC - 1 + 3)

    def remote(src, dst, ss, rs, where):
        return pltpu.make_async_remote_copy(
            src_ref=src, dst_ref=dst, send_sem=ss, recv_sem=rs, device_id=where, device_id_type=MESH
        )

    def piece(ref, c):
        return ref.at[:, pl.ds(pl.multiple_of(16 * lax.rem(c, 4), 16), 16), pl.ds(pl.multiple_of(128 * lax.div(c, 4), 128), 128)]

    def octet(ref, c):
        return ref.at[:, pl.ds(pl.multiple_of(8 * lax.rem(c, 8), 8), 8), :]

    my_slots = pl.ds(BPD * me, BPD)

    def small_source(c, act):
        @pl.when(c < 8)
        def _():
            act(octet(keys, c))

        @pl.when((c >= 8) & (c < 16))
        def _():
            act(octet(queries, c))

    def step_source(c, act):
        @pl.when((c >= 16) & (c < 24))
        def _():
            act(octet(step_pad, c))

    def first_v(d, carry):
        c = peer(d)
        where = {"ctx": c}
        small_source(c, lambda src: remote(src, recv_s.at[my_slots], k_send, k_recv, where).start())
        remote(piece(values, c), recv_v.at[my_slots], v_send, v_recv, where).start()
        return carry

    lax.fori_loop(1, NC, first_v, 0)
    small_source(me, lambda src: pltpu.make_async_copy(src, recv_s.at[my_slots], k_recv).start())
    pltpu.make_async_copy(piece(values, me), recv_v.at[my_slots], v_recv).start()

    for load in loads:
        load.wait()
    wide = jnp.concatenate(
        [steps_in[...].astype(F32), jnp.zeros((128 - HEADS, SPAN), F32)], axis=0
    )
    step_pad[...] = jnp.transpose(wide).astype(BF16).reshape(BPD, BLK, 128)
    rows16[...] = jnp.zeros_like(rows16)
    rows16[0:1, 0:HEADS] = step_bias[...]
    rows16[1:2, 0:HEADS] = decay_log[...]
    side = (NC * BPD, NC * BPD)
    placed = jnp.transpose(jnp.broadcast_to(order[...], side))
    found_at = jnp.where(placed == iota(side, 1), iota(side, 0), 0)
    inv_row[0:1, :] = jnp.max(found_at, axis=0, keepdims=True)
    inv_copy = pltpu.make_async_copy(inv_row, inv, inv_sem)
    inv_copy.start()

    def first_step(c, carry):
        @pl.when(c != me)
        def _():
            remote(octet(step_pad, c), recv_s.at[my_slots], k_send, k_recv, {"ctx": c}).start()

        return carry

    lax.fori_loop(16, 24, first_step, 0)
    step_source(me, lambda src: pltpu.make_async_copy(src, recv_s.at[my_slots], k_recv).start())

    def first_g(d, carry):
        c = peer(d)
        remote(piece(gates, c), recv_g.at[my_slots], g_send, g_recv, {"ctx": c}).start()
        return carry

    lax.fori_loop(1, FIRST_G, first_g, 0)
    weight_copy = pltpu.make_async_copy(weight_hbm, weight, w_sem)
    weight_copy.start()
    inv_copy.wait()

    starts = []
    total = jnp.int32(0)
    for k in range(DOCS):
        starts.append(total - me * SPAN)
        total = total + doc_lengths[0, k]

    row = iota((SPAN, 128), 0)

    def opening_at(position):
        hit = position == starts[0]
        for k in range(1, DOCS):
            hit = hit | (position == starts[k])
        return hit

    open0 = opening_at(row)
    open1 = opening_at(row - 1)
    open2 = opening_at(row - 2)
    masks[0] = jnp.where(open0 | open1 | open2, 0.0, 1.0).astype(F32)
    masks[1] = jnp.where(open0 | open1, 0.0, 1.0).astype(F32)
    masks[2] = jnp.where(open0, 0.0, 1.0).astype(F32)

    tail_cut = jnp.zeros((SPAN, 128), jnp.int32)
    head_cut = jnp.zeros((SPAN, 128), jnp.int32)
    for k in range(DOCS):
        inside = (row * 0 + starts[k] >= 0) & (row * 0 + starts[k] < SPAN)
        tail_cut = tail_cut | jnp.where(inside & (row < starts[k]), 1, 0)
        head_cut = head_cut | jnp.where(inside & (row >= starts[k]), 1, 0)

    def owner_slots(o):
        return pl.ds(BPD * o, BPD)

    def fill(src, dst, o):
        for k in range(BPD):
            dst[BPD * o + k] = src[inv[0, BPD * o + k]]

    def before(o):
        return inv[0, lax.rem(BPD * o + NC * BPD - 1, NC * BPD)]

    has_small = me < 24
    kind = lax.div(me, 8)

    def small_target(i):
        return main_s.at[i, :, pl.ds(pl.multiple_of(8 * lax.rem(me, 8), 8), 8), :]

    @pl.when(has_small)
    def _():
        pltpu.make_async_copy(recv_s, recv_s, k_recv).wait()
        sends_rim = (lax.rem(me, 8) == 7) & (me < 16)

        def second_s(d, carry):
            o = peer(d)
            where = {"ctx": o}
            fill(recv_s, send_s, o)
            remote(send_s.at[owner_slots(o)], small_target(kind), k2_send, k2_recv, where).start()

            @pl.when(sends_rim)
            def _():
                rim_send_s[o] = recv_s[before(o)]
                remote(rim_send_s.at[o], rim_s.at[kind], rk_send, rk_recv, where).start()

            return carry

        lax.fori_loop(1, NC, second_s, 0)
        fill(recv_s, send_s, me)
        pltpu.make_async_copy(send_s.at[owner_slots(me)], small_target(kind), k2_recv).start()

        @pl.when(sends_rim)
        def _():
            rim_send_s[me] = recv_s[before(me)]
            pltpu.make_async_copy(rim_send_s.at[me], rim_s.at[kind], rk_recv).start()

    pltpu.make_async_copy(recv_v, recv_v, v_recv).wait()
    v_rim = lax.rem(me, 4) == 3

    def rim_target():
        return rim_v.at[:, pl.ds(pl.multiple_of(128 * lax.div(me, 4), 128), 128)]

    def second_v(d, carry):
        o = peer(d)
        where = {"ctx": o}
        fill(recv_v, send_v, o)
        remote(send_v.at[owner_slots(o)], piece(main_v, me), v2_send, v2_recv, where).start()

        @pl.when(v_rim)
        def _():
            rim_send_v[o] = recv_v[before(o)]
            remote(rim_send_v.at[o], rim_target(), rv_send, rv_recv, where).start()

        return carry

    lax.fori_loop(1, NC, second_v, 0)
    fill(recv_v, send_v, me)
    pltpu.make_async_copy(send_v.at[owner_slots(me)], piece(main_v, me), v2_recv).start()

    @pl.when(v_rim)
    def _():
        rim_send_v[me] = recv_v[before(me)]
        pltpu.make_async_copy(rim_send_v.at[me], rim_target(), rv_recv).start()

    lax.fori_loop(FIRST_G, NC, first_g, 0)
    pltpu.make_async_copy(piece(gates, me), recv_g.at[my_slots], g_recv).start()

    pltpu.make_async_copy(main_s, main_s, k2_recv).wait()
    pltpu.make_async_copy(rim_s, rim_s, rk_recv).wait()

    def conv(rim, rows, taps):
        ext = jnp.concatenate([rim, rows], axis=0)
        acc = (masks[0] * taps[0:1, :]) * pltpu.roll(ext, 3, 0)[8:, :]
        acc = acc + (masks[1] * taps[1:2, :]) * pltpu.roll(ext, 2, 0)[8:, :]
        acc = acc + (masks[2] * taps[2:3, :]) * pltpu.roll(ext, 1, 0)[8:, :]
        acc = acc + taps[3:4, :] * rows
        return silu(acc)

    key_f = conv(rim_s[0].astype(F32), main_s[0].reshape(SPAN, 128).astype(F32), taps_k)
    query_f = conv(rim_s[1].astype(F32), main_s[1].reshape(SPAN, 128).astype(F32), taps_q)
    conv_k[...] = key_f.astype(BF16)
    conv_q[...] = query_f.astype(BF16)

    pre = main_s[2].reshape(SPAN, 128).astype(F32) + rows16[0:1, :]
    small = jnp.exp(-jnp.abs(pre))
    one_more = 1.0 + small
    gap = one_more - 1.0
    log1p = jnp.where(gap == 0.0, small, jnp.log(one_more) * small / jnp.where(gap == 0.0, 1.0, gap))
    step = jnp.maximum(pre, 0.0) + log1p
    sums = -jnp.exp(rows16[1:2, :]) * step
    for k in (1, 2, 4, 8, 16, 32, 64, 128):
        sums = sums + jnp.where(row >= k, pltpu.roll(sums, k, 0), 0.0)
    last = sums[SPAN - 1 : SPAN, :]
    tail = jnp.where(tail_cut > 0, 0.0, jnp.exp(last - sums) * step)
    inflow = jnp.where(head_cut > 0, 0.0, jnp.exp(sums))
    spread = jnp.where(
        lax.div(iota((128, WIDTH), 1), 64) == iota((128, WIDTH), 0), 1.0, 0.0
    ).astype(F32)
    tail_x[...] = jnp.dot(tail, spread, precision=HIGHEST, preferred_element_type=F32)
    inflow_x[...] = jnp.dot(inflow, spread, precision=HIGHEST, preferred_element_type=F32)
    gate_row = inflow_x[SPAN - 1 : SPAN, :]
    gate_hi = gate_row.astype(BF16)
    gate_lo = (gate_row - gate_hi.astype(F32)).astype(BF16)
    which = iota((8, WIDTH), 0)
    gate_rows = jnp.where(
        which == 0, gate_hi.astype(F32), jnp.where(which == 1, gate_lo.astype(F32), 0.0)
    ).astype(BF16)
    sums_t = jnp.transpose(sums)
    step_t = jnp.transpose(step)
    key_t = jnp.transpose(conv_k[...].astype(F32)).astype(BF16)
    t_id = iota((SPAN, SPAN), 0)
    u_id = iota((SPAN, SPAN), 1)
    drop = u_id > t_id
    for k in range(DOCS):
        drop = drop | ((u_id < starts[k]) & (t_id >= starts[k]))
    inner = lax.dot_general(
        conv_q[...], conv_k[...], (((1,), (1,)), ((), ())), preferred_element_type=F32
    )
    product[...] = jnp.where(drop, 0.0, inner)

    pltpu.make_async_copy(main_v, main_v, v2_recv).wait()
    pltpu.make_async_copy(rim_v, rim_v, rv_recv).wait()
    for g in range(8):
        lanes = slice(128 * g, 128 * g + 128)
        rows = main_v[:, :, lanes].reshape(SPAN, 128).astype(F32)
        rim = rim_v[:, lanes].astype(F32)[8:16, :]
        conv_v[:, lanes] = conv(rim, rows, taps_v[:, lanes]).astype(BF16)

    scaled = (conv_v[...].astype(F32) * tail_x[...]).astype(BF16)
    local = jnp.dot(key_t, scaled, preferred_element_type=F32).astype(BF16)
    for r in range(4):
        st_send[r, 0:32, :] = local[32 * r : 32 * r + 32, :]
        st_send[r, 32:40, :] = gate_rows

    def state_piece(c):
        return st_send.at[lax.rem(c, 4), :, pl.ds(pl.multiple_of(128 * lax.div(c, 4), 128), 128)]

    def send_state(d, carry):
        c = peer(d)
        remote(state_piece(c), st_recv.at[me], st_ss, st_rs, {"ctx": c}).start()
        return carry

    pltpu.make_async_copy(state_piece(me), st_recv.at[me], st_rs).start()
    lax.fori_loop(1, NC, send_state, 0)

    def half_piece(half):
        return piece(main_g.at[pl.ds(2 * half, 2)], me)

    def half_slots(o, half):
        return pl.ds(BPD * o + 2 * half, 2)

    def second_g(half):
        def one(d, carry):
            o = peer(d)
            for k in range(2 * half, 2 * half + 2):
                send_g[BPD * o + k] = recv_g[inv[0, BPD * o + k]]
            src = send_g.at[half_slots(o, half)]
            remote(src, half_piece(half), g2_send.at[half], g2_recv.at[half], {"ctx": o}).start()
            return carry

        lax.fori_loop(1, NC, one, 0)
        for k in range(2 * half, 2 * half + 2):
            send_g[BPD * me + k] = recv_g[inv[0, BPD * me + k]]
        src = send_g.at[half_slots(me, half)]
        pltpu.make_async_copy(src, half_piece(half), g2_recv.at[half]).start()

    left = iota((SPAN, 128), 1) < 64

    def intra(g):
        lanes = slice(128 * g, 128 * g + 128)
        pair = conv_v[:, lanes]
        found = []
        for h in (2 * g, 2 * g + 1):
            decay = jnp.exp(jnp.minimum(sums[:, h : h + 1] - sums_t[h : h + 1, :], 0.0))
            mix = (decay * (product[...] * step_t[h : h + 1, :])).astype(BF16)
            found.append(jnp.dot(mix, pair, preferred_element_type=F32))
        gain = jnp.where(left, skip[0, 2 * g], skip[0, 2 * g + 1])
        y[:, lanes] = jnp.where(left, found[0], found[1]) + gain * pair.astype(F32)

    for g in range(3):
        intra(g)

    pltpu.make_async_copy(recv_g, recv_g, g_recv).wait()
    second_g(0)

    for g in range(3, 6):
        intra(g)

    pltpu.make_async_copy(st_recv, st_recv, st_rs).wait()
    state = jnp.zeros((32, 128), F32)
    for o in range(NC):
        ent_send[o] = state.astype(BF16)
        part = st_recv[o, 0:32, :].astype(F32)
        pair = st_recv[o, 32:40, :].astype(F32)
        state = (pair[0:1, :] + pair[1:2, :]) * state + part

    def ent_target():
        return ent.at[pl.ds(pl.multiple_of(32 * lax.rem(me, 4), 32), 32), pl.ds(pl.multiple_of(128 * lax.div(me, 4), 128), 128)]

    def send_ent(d, carry):
        o = peer(d)
        remote(ent_send.at[o], ent_target(), en_ss, en_rs, {"ctx": o}).start()
        return carry

    pltpu.make_async_copy(ent_send.at[me], ent_target(), en_rs).start()
    lax.fori_loop(1, NC, send_ent, 0)

    second_g(1)

    for g in range(6, 8):
        intra(g)

    pltpu.make_async_copy(ent, ent, en_rs).wait()
    for g in range(8):
        lanes = slice(128 * g, 128 * g + 128)
        carried = jnp.dot(conv_q[...], ent[:, lanes], preferred_element_type=F32)
        y[:, lanes] = y[:, lanes] + inflow_x[:, lanes] * carried

    def s1_copy(half, i):
        return remote(
            s1_send.at[half, i], s1_recv.at[half, i], s1_ss.at[half, i], s1_rs.at[half, i], {"tp": sibling}
        )

    def pair_copy(half, i):
        return remote(
            pair_send.at[half, i], pair_recv.at[half, i], p_ss.at[half, i], p_rs.at[half, i], {"tp": partner}
        )

    def last_copy(half, i):
        return remote(last_send.at[i], last_recv.at[i], l_ss.at[i], l_rs.at[i], {"tp": across})

    for half in range(2):
        rows = slice(128 * half, 128 * half + 128)
        wait_g = main_g.at[pl.ds(2 * half, 2)]
        pltpu.make_async_copy(wait_g, wait_g, g2_recv.at[half]).wait()
        squares = jnp.zeros((128, 128), F32)
        for g in range(8):
            lanes = slice(128 * g, 128 * g + 128)
            gate = main_g[2 * half : 2 * half + 2, :, lanes].reshape(128, 128).astype(F32)
            gated = y[rows, lanes] * silu(gate)
            squares = squares + gated * gated
            y[rows, lanes] = gated
        mean = jnp.sum(squares, axis=1, keepdims=True) * (1.0 / WIDTH)
        scale = lax.rsqrt(mean + 1e-05)
        normed[rows, :] = (y[rows, :] * scale * norm_gain[...]).astype(BF16)
        if half == 0:
            weight_copy.wait()
        sends = lax.div(my_x, 2) if half == 0 else 1 - lax.div(my_x, 2)
        mine = parity + sends - 2 * parity * sends
        for i in range(NCHUNK + 2):
            if i < NCHUNK:
                part = jnp.dot(
                    normed[rows, :], weight[:, CW * i : CW * i + CW], preferred_element_type=F32
                )
                own_part[...] = part.reshape(2, 2, 32, CW)
                s1_send[half, i] = own_part[:, 1 - core].astype(BF16)
                s1_copy(half, i).start()
                keep[half, i] = own_part[:, core]
            if 1 <= i <= NCHUNK:
                k = i - 1
                s1_copy(half, k).wait_recv()
                keep[half, k] = keep[half, k] + s1_recv[half, k].astype(F32)
                pair_send[half, k] = keep[half, k, 1 - mine].astype(BF16)
                pair_copy(half, k).start()
            if i >= 2:
                k = i - 2
                pair_copy(half, k).wait_recv()
                both = keep[half, k, mine] + pair_recv[half, k].astype(F32)
                keep[half, k, 0] = both

                @pl.when(sends == 1)
                def _():
                    last_send[k] = keep[half, k, 0].astype(BF16)
                    last_copy(half, k).start()

    for half in range(2):
        sends = lax.div(my_x, 2) if half == 0 else 1 - lax.div(my_x, 2)

        @pl.when(sends == 0)
        def _():
            for i in range(NCHUNK):
                last_copy(half, i).wait_recv()
                both = keep[half, i, 0] + last_recv[i].astype(F32)
                out[:, CW * i : CW * i + CW] = both.astype(BF16)

    most = pl.ds(0, BPD * (NC - 1))
    for ref, sem in ((recv_v, v_send), (recv_g, g_send), (send_v, v2_send)):
        pltpu.make_async_copy(ref.at[most], ref.at[most], sem).wait()

    @pl.when(me < 24)
    def _():
        some = recv_s.at[pl.ds(0, BPD * 23)]
        pltpu.make_async_copy(some, some, k_send).wait()
        some = send_s.at[most]
        pltpu.make_async_copy(some, some, k2_send).wait()

    @pl.when(me >= 24)
    def _():
        some = recv_s.at[pl.ds(0, BPD * 24)]
        pltpu.make_async_copy(some, some, k_send).wait()

    @pl.when(v_rim)
    def _():
        some = rim_send_v.at[pl.ds(0, NC - 1)]
        pltpu.make_async_copy(some, some, rv_send).wait()

    @pl.when((lax.rem(me, 8) == 7) & (me < 16))
    def _():
        some = rim_send_s.at[pl.ds(0, NC - 1)]
        pltpu.make_async_copy(some, some, rk_send).wait()

    for half in range(2):
        some = send_g.at[pl.ds(0, 2 * (NC - 1))]
        pltpu.make_async_copy(some, some, g2_send.at[half]).wait()
    some = st_recv.at[pl.ds(0, NC - 1)]
    pltpu.make_async_copy(some, some, st_ss).wait()
    some = ent_send.at[pl.ds(0, NC - 1)]
    pltpu.make_async_copy(some, some, en_ss).wait()
    for i in range(NCHUNK):
        for half in range(2):
            s1_copy(half, i).wait_send()
            pair_copy(half, i).wait_send()
        last_copy(0, i).wait_send()


def on_device(
    values_in,
    gate_in,
    keys_in,
    queries_in,
    step_in,
    block_order,
    doc_lengths,
    conv_values,
    conv_keys,
    conv_queries,
    decay_log,
    step_bias,
    skip_gain,
    norm_gain,
    out_weight,
):
    count = NC * BPD
    vmem = pl.BlockSpec(memory_space=pltpu.VMEM)
    hbm = pl.BlockSpec(memory_space=pltpu.HBM)
    dma = pltpu.SemaphoreType.DMA
    scratch = [
        pltpu.VMEM((1, count), jnp.int32),
        pltpu.SMEM((1, DOCS), jnp.int32),
        pltpu.SMEM((1, HEADS), F32),
        pltpu.VMEM((HEADS, SPAN), BF16),
        pltpu.VMEM((4, WIDTH), F32),
        pltpu.VMEM((4, STATE), F32),
        pltpu.VMEM((4, STATE), F32),
        pltpu.VMEM((1, HEADS), F32),
        pltpu.VMEM((1, HEADS), F32),
        pltpu.VMEM((1, WIDTH), F32),
        pltpu.VMEM((1, count), jnp.int32),
        pltpu.SMEM((1, count), jnp.int32),
        dma((10,)),
        dma(()),
        pltpu.VMEM((WIDTH, OUTW), BF16),
        pltpu.VMEM((BPD, BLK, 128), BF16),
        pltpu.VMEM((8, 128), F32),
        pltpu.VMEM((count, 16, 128), BF16),
        pltpu.VMEM((count, 16, 128), BF16),
        pltpu.VMEM((count, 8, 128), BF16),
        pltpu.VMEM((count, 16, 128), BF16),
        pltpu.VMEM((count, 16, 128), BF16),
        pltpu.VMEM((count, 8, 128), BF16),
        pltpu.VMEM((BPD, BLK, WIDTH), BF16),
        pltpu.VMEM((BPD, BLK, WIDTH), BF16),
        pltpu.VMEM((3, BPD, BLK, 128), BF16),
        pltpu.VMEM((16, WIDTH), BF16),
        pltpu.VMEM((2, 8, 128), BF16),
        pltpu.VMEM((NC, 16, 128), BF16),
        pltpu.VMEM((NC, 8, 128), BF16),
        pltpu.VMEM((SPAN, WIDTH), BF16),
        pltpu.VMEM((SPAN, STATE), BF16),
        pltpu.VMEM((SPAN, STATE), BF16),
        pltpu.VMEM((3, SPAN, 128), F32),
        pltpu.VMEM((SPAN, SPAN), F32),
        pltpu.VMEM((SPAN, WIDTH), F32),
        pltpu.VMEM((SPAN, WIDTH), F32),
        pltpu.VMEM((4, 40, WIDTH), BF16),
        pltpu.VMEM((NC, 40, 128), BF16),
        pltpu.VMEM((NC, 32, 128), BF16),
        pltpu.VMEM((STATE, WIDTH), BF16),
        pltpu.VMEM((SPAN, WIDTH), F32),
        pltpu.VMEM((SPAN, WIDTH), BF16),
        pltpu.VMEM((2, NCHUNK, 2, 32, CW), BF16),
        pltpu.VMEM((2, NCHUNK, 2, 32, CW), BF16),
        pltpu.VMEM((2, 2, 32, CW), F32),
        pltpu.VMEM((2, NCHUNK, 2, 32, CW), F32),
        pltpu.VMEM((2, NCHUNK, 32, CW), BF16),
        pltpu.VMEM((2, NCHUNK, 32, CW), BF16),
        pltpu.VMEM((NCHUNK, 32, CW), BF16),
        pltpu.VMEM((NCHUNK, 32, CW), BF16),
        dma(()),
    ]
    scratch += [dma(()) for _ in range(6)] + [dma(()), dma(())] + [dma((2,)), dma((2,))]
    scratch += [dma(()) for _ in range(6)]
    scratch += [dma(()) for _ in range(4)]
    scratch += [dma((2, NCHUNK)) for _ in range(4)] + [dma((NCHUNK,)), dma((NCHUNK,))]
    call = pl.pallas_call(
        body,
        out_shape=jax.ShapeDtypeStruct((SPAN // 8, OUTW), BF16),
        in_specs=[hbm] * 15,
        out_specs=vmem,
        scratch_shapes=scratch,
        compiler_params=pltpu.CompilerParams(
            collective_id=0, has_side_effects=True, vmem_limit_bytes=60 << 20
        ),
        name="layer",
    )
    return call(
        block_order.reshape(1, count),
        doc_lengths.reshape(1, DOCS),
        skip_gain.reshape(1, HEADS),
        values_in.reshape(BPD, BLK, WIDTH),
        gate_in.reshape(BPD, BLK, WIDTH),
        keys_in.reshape(BPD, BLK, STATE),
        queries_in.reshape(BPD, BLK, STATE),
        step_in.T,
        conv_values,
        conv_keys,
        conv_queries,
        decay_log.reshape(1, HEADS),
        step_bias.reshape(1, HEADS),
        norm_gain.reshape(1, WIDTH),
        out_weight,
    )


def solution(mesh):
    in_specs = (
        P("ctx", "tp"),
        P("ctx", "tp"),
        P("ctx", "tp"),
        P("ctx", "tp"),
        P("ctx", "tp"),
        P(),
        P(),
        P(None, "tp"),
        P(None, "tp"),
        P(None, "tp"),
        P("tp"),
        P("tp"),
        P("tp"),
        P("tp"),
        P("tp", None),
    )
    out_specs = P(("ctx", "tp"), None)
    return jax.shard_map(
        on_device, mesh=mesh, in_specs=in_specs, out_specs=out_specs, check_vma=False
    )
```

```python
import functools

import jax
import jax.numpy as jnp
from jax import lax
from jax.experimental import pallas as pl
from jax.experimental.pallas import tpu as pltpu
from jax.sharding import PartitionSpec as P

NC = 32
BPD = 4
BLK = 64
SPAN = 256
WIDTH = 1024
HEADS = 16
STATE = 128
OUTW = 4096
DOCS = 16
NCHUNK = 4
CW = OUTW // NCHUNK
FIRST_G = 12
MESH = pl.DeviceIdType.MESH
F32 = jnp.float32
BF16 = jnp.bfloat16
HIGHEST = lax.Precision.HIGHEST


def silu(x):
    return x * jax.nn.sigmoid(x)


def iota(shape, axis):
    return lax.broadcasted_iota(jnp.int32, shape, axis)


def body(
    order_hbm,
    lengths_hbm,
    skip_hbm,
    values,
    gates,
    keys,
    queries,
    steps_hbm,
    taps_v_hbm,
    taps_k_hbm,
    taps_q_hbm,
    decay_hbm,
    bias_hbm,
    gain_hbm,
    weight_hbm,
    out,
    order,
    doc_lengths,
    skip,
    steps_in,
    taps_v,
    taps_k,
    taps_q,
    decay_log,
    step_bias,
    norm_gain,
    inv_row,
    inv,
    local_sem,
    inv_sem,
    weight,
    step_pad,
    rows16,
    recv_v,
    recv_g,
    recv_s,
    send_v,
    send_g,
    send_s,
    main_v,
    main_g,
    main_s,
    rim_v,
    rim_s,
    rim_send_v,
    rim_send_s,
    conv_v,
    conv_k,
    conv_q,
    masks,
    product,
    tail_x,
    inflow_x,
    st_send,
    st_recv,
    ent_send,
    ent,
    y,
    normed,
    s1_send,
    s1_recv,
    own_part,
    keep,
    s2_send,
    s2_recv,
    w_sem,
    v_send,
    v_recv,
    g_send,
    g_recv,
    k_send,
    k_recv,
    v2_send,
    v2_recv,
    g2_send,
    g2_recv,
    k2_send,
    k2_recv,
    rv_send,
    rv_recv,
    rk_send,
    rk_recv,
    st_ss,
    st_rs,
    en_ss,
    en_rs,
    s1_ss,
    s1_rs,
    s2_ss,
    s2_rs,
):
    me = lax.axis_index("ctx")
    tp = lax.axis_index("tp")
    my_x = lax.div(tp, 2)
    core = lax.rem(tp, 2)
    sibling = my_x * 2 + (1 - core)

    loads = [
        pltpu.make_async_copy(src, dst, local_sem.at[i])
        for i, (src, dst) in enumerate(
            (
                (steps_hbm, steps_in),
                (order_hbm, order),
                (lengths_hbm, doc_lengths),
                (skip_hbm, skip),
                (taps_v_hbm, taps_v),
                (taps_k_hbm, taps_k),
                (taps_q_hbm, taps_q),
                (decay_hbm, decay_log),
                (bias_hbm, step_bias),
                (gain_hbm, norm_gain),
            )
        )
    ]
    barrier = pltpu.get_barrier_semaphore()

    def peer(d):
        return lax.rem(me + d, NC)

    def greet(d, carry):
        pl.semaphore_signal(barrier, inc=1, device_id={"ctx": peer(d)}, device_id_type=MESH)
        return carry

    lax.fori_loop(1, NC, greet, 0)
    pl.semaphore_signal(barrier, inc=1, device_id={"tp": sibling}, device_id_type=MESH)
    for dx in range(1, 4):
        other = lax.rem(my_x + dx, 4) * 2 + core
        pl.semaphore_signal(barrier, inc=1, device_id={"tp": other}, device_id_type=MESH)

    for load in loads:
        load.start()
    pl.semaphore_wait(barrier, NC - 1 + 4)

    def remote(src, dst, ss, rs, where):
        return pltpu.make_async_remote_copy(
            src_ref=src, dst_ref=dst, send_sem=ss, recv_sem=rs, device_id=where, device_id_type=MESH
        )

    def piece(ref, c):
        return ref.at[:, pl.ds(pl.multiple_of(16 * lax.rem(c, 4), 16), 16), pl.ds(pl.multiple_of(128 * lax.div(c, 4), 128), 128)]

    def octet(ref, c):
        return ref.at[:, pl.ds(pl.multiple_of(8 * lax.rem(c, 8), 8), 8), :]

    my_slots = pl.ds(BPD * me, BPD)

    def gate_piece(ref, c, half):
        turn = lax.rem(c, 4)
        lanes = pl.ds(pl.multiple_of(128 * lax.div(c, 4), 128), 128)
        return ref.at[:, lax.div(turn, 2), half, lax.rem(turn, 2), :, lanes]


    def small_source(c, act):
        @pl.when(c < 8)
        def _():
            act(octet(keys, c))

        @pl.when((c >= 8) & (c < 16))
        def _():
            act(octet(queries, c))

    def step_source(c, act):
        @pl.when((c >= 16) & (c < 24))
        def _():
            act(octet(step_pad, c))

    def first_v(d, carry):
        c = peer(d)
        where = {"ctx": c}
        small_source(c, lambda src: remote(src, recv_s.at[my_slots], k_send, k_recv, where).start())
        remote(piece(values, c), recv_v.at[my_slots], v_send, v_recv, where).start()
        return carry

    lax.fori_loop(1, NC, first_v, 0)
    small_source(me, lambda src: pltpu.make_async_copy(src, recv_s.at[my_slots], k_recv).start())
    pltpu.make_async_copy(piece(values, me), recv_v.at[my_slots], v_recv).start()

    for load in loads:
        load.wait()
    wide = jnp.concatenate(
        [steps_in[...].astype(F32), jnp.zeros((128 - HEADS, SPAN), F32)], axis=0
    )
    step_pad[...] = jnp.transpose(wide).astype(BF16).reshape(BPD, BLK, 128)
    rows16[...] = jnp.zeros_like(rows16)
    rows16[0:1, 0:HEADS] = step_bias[...]
    rows16[1:2, 0:HEADS] = decay_log[...]
    side = (NC * BPD, NC * BPD)
    placed = jnp.transpose(jnp.broadcast_to(order[...], side))
    found_at = jnp.where(placed == iota(side, 1), iota(side, 0), 0)
    inv_row[0:1, :] = jnp.max(found_at, axis=0, keepdims=True)
    inv_copy = pltpu.make_async_copy(inv_row, inv, inv_sem)
    inv_copy.start()

    def first_step(c, carry):
        @pl.when(c != me)
        def _():
            remote(octet(step_pad, c), recv_s.at[my_slots], k_send, k_recv, {"ctx": c}).start()

        return carry

    lax.fori_loop(16, 24, first_step, 0)
    step_source(me, lambda src: pltpu.make_async_copy(src, recv_s.at[my_slots], k_recv).start())

    def first_g(d, carry):
        c = peer(d)
        remote(gate_piece(gates, c, slice(None)), recv_g.at[my_slots], g_send, g_recv, {"ctx": c}).start()
        return carry

    lax.fori_loop(1, FIRST_G, first_g, 0)
    weight_copy = pltpu.make_async_copy(weight_hbm, weight, w_sem)
    weight_copy.start()
    inv_copy.wait()

    starts = []
    total = jnp.int32(0)
    for k in range(DOCS):
        starts.append(total - me * SPAN)
        total = total + doc_lengths[0, k]

    row = iota((SPAN, 128), 0)

    def opening_at(position):
        hit = position == starts[0]
        for k in range(1, DOCS):
            hit = hit | (position == starts[k])
        return hit

    open0 = opening_at(row)
    open1 = opening_at(row - 1)
    open2 = opening_at(row - 2)
    masks[0] = jnp.where(open0 | open1 | open2, 0.0, 1.0).astype(F32)
    masks[1] = jnp.where(open0 | open1, 0.0, 1.0).astype(F32)
    masks[2] = jnp.where(open0, 0.0, 1.0).astype(F32)

    tail_cut = jnp.zeros((SPAN, 128), jnp.int32)
    head_cut = jnp.zeros((SPAN, 128), jnp.int32)
    for k in range(DOCS):
        inside = (row * 0 + starts[k] >= 0) & (row * 0 + starts[k] < SPAN)
        tail_cut = tail_cut | jnp.where(inside & (row < starts[k]), 1, 0)
        head_cut = head_cut | jnp.where(inside & (row >= starts[k]), 1, 0)

    def owner_slots(o):
        return pl.ds(BPD * o, BPD)

    def fill(src, dst, o):
        for k in range(BPD):
            dst[BPD * o + k] = src[inv[0, BPD * o + k]]

    def before(o):
        return inv[0, lax.rem(BPD * o + NC * BPD - 1, NC * BPD)]

    has_small = me < 24
    kind = lax.div(me, 8)

    def small_target(i):
        return main_s.at[i, :, pl.ds(pl.multiple_of(8 * lax.rem(me, 8), 8), 8), :]

    @pl.when(has_small)
    def _():
        pltpu.make_async_copy(recv_s, recv_s, k_recv).wait()
        sends_rim = (lax.rem(me, 8) == 7) & (me < 16)

        def second_s(d, carry):
            o = peer(d)
            where = {"ctx": o}
            fill(recv_s, send_s, o)
            remote(send_s.at[owner_slots(o)], small_target(kind), k2_send, k2_recv, where).start()

            @pl.when(sends_rim)
            def _():
                rim_send_s[o] = recv_s[before(o)]
                remote(rim_send_s.at[o], rim_s.at[kind], rk_send, rk_recv, where).start()

            return carry

        lax.fori_loop(1, NC, second_s, 0)
        fill(recv_s, send_s, me)
        pltpu.make_async_copy(send_s.at[owner_slots(me)], small_target(kind), k2_recv).start()

        @pl.when(sends_rim)
        def _():
            rim_send_s[me] = recv_s[before(me)]
            pltpu.make_async_copy(rim_send_s.at[me], rim_s.at[kind], rk_recv).start()

    pltpu.make_async_copy(recv_v, recv_v, v_recv).wait()
    v_rim = lax.rem(me, 4) == 3

    def rim_target():
        return rim_v.at[:, pl.ds(pl.multiple_of(128 * lax.div(me, 4), 128), 128)]

    def second_v(d, carry):
        o = peer(d)
        where = {"ctx": o}
        fill(recv_v, send_v, o)
        remote(send_v.at[owner_slots(o)], piece(main_v, me), v2_send, v2_recv, where).start()

        @pl.when(v_rim)
        def _():
            rim_send_v[o] = recv_v[before(o)]
            remote(rim_send_v.at[o], rim_target(), rv_send, rv_recv, where).start()

        return carry

    lax.fori_loop(1, NC, second_v, 0)
    fill(recv_v, send_v, me)
    pltpu.make_async_copy(send_v.at[owner_slots(me)], piece(main_v, me), v2_recv).start()

    @pl.when(v_rim)
    def _():
        rim_send_v[me] = recv_v[before(me)]
        pltpu.make_async_copy(rim_send_v.at[me], rim_target(), rv_recv).start()

    lax.fori_loop(FIRST_G, NC, first_g, 0)
    pltpu.make_async_copy(gate_piece(gates, me, slice(None)), recv_g.at[my_slots], g_recv).start()

    pltpu.make_async_copy(main_s, main_s, k2_recv).wait()
    pltpu.make_async_copy(rim_s, rim_s, rk_recv).wait()

    def conv(rim, rows, taps):
        ext = jnp.concatenate([rim, rows], axis=0)
        acc = (masks[0] * taps[0:1, :]) * pltpu.roll(ext, 3, 0)[8:, :]
        acc = acc + (masks[1] * taps[1:2, :]) * pltpu.roll(ext, 2, 0)[8:, :]
        acc = acc + (masks[2] * taps[2:3, :]) * pltpu.roll(ext, 1, 0)[8:, :]
        acc = acc + taps[3:4, :] * rows
        return silu(acc)

    key_f = conv(rim_s[0].astype(F32), main_s[0].reshape(SPAN, 128).astype(F32), taps_k)
    query_f = conv(rim_s[1].astype(F32), main_s[1].reshape(SPAN, 128).astype(F32), taps_q)
    conv_k[...] = key_f.astype(BF16)
    conv_q[...] = query_f.astype(BF16)

    pre = main_s[2].reshape(SPAN, 128).astype(F32) + rows16[0:1, :]
    small = jnp.exp(-jnp.abs(pre))
    one_more = 1.0 + small
    gap = one_more - 1.0
    log1p = jnp.where(gap == 0.0, small, jnp.log(one_more) * small / jnp.where(gap == 0.0, 1.0, gap))
    step = jnp.maximum(pre, 0.0) + log1p
    sums = -jnp.exp(rows16[1:2, :]) * step
    for k in (1, 2, 4, 8, 16, 32, 64, 128):
        sums = sums + jnp.where(row >= k, pltpu.roll(sums, k, 0), 0.0)
    last = sums[SPAN - 1 : SPAN, :]
    tail = jnp.where(tail_cut > 0, 0.0, jnp.exp(last - sums) * step)
    inflow = jnp.where(head_cut > 0, 0.0, jnp.exp(sums))
    spread = jnp.where(
        lax.div(iota((128, WIDTH), 1), 64) == iota((128, WIDTH), 0), 1.0, 0.0
    ).astype(F32)
    tail_x[...] = jnp.dot(tail, spread, precision=HIGHEST, preferred_element_type=F32)
    inflow_x[...] = jnp.dot(inflow, spread, precision=HIGHEST, preferred_element_type=F32)
    gate_row = inflow_x[SPAN - 1 : SPAN, :]
    gate_hi = gate_row.astype(BF16)
    gate_lo = (gate_row - gate_hi.astype(F32)).astype(BF16)
    which = iota((8, WIDTH), 0)
    gate_rows = jnp.where(
        which == 0, gate_hi.astype(F32), jnp.where(which == 1, gate_lo.astype(F32), 0.0)
    ).astype(BF16)
    sums_t = jnp.transpose(sums)
    step_t = jnp.transpose(step)
    key_t = jnp.transpose(conv_k[...].astype(F32)).astype(BF16)
    t_id = iota((SPAN, SPAN), 0)
    u_id = iota((SPAN, SPAN), 1)
    drop = u_id > t_id
    for k in range(DOCS):
        drop = drop | ((u_id < starts[k]) & (t_id >= starts[k]))
    inner = lax.dot_general(
        conv_q[...], conv_k[...], (((1,), (1,)), ((), ())), preferred_element_type=F32
    )
    product[...] = jnp.where(drop, 0.0, inner)

    pltpu.make_async_copy(main_v, main_v, v2_recv).wait()
    pltpu.make_async_copy(rim_v, rim_v, rv_recv).wait()
    for g in range(8):
        lanes = slice(128 * g, 128 * g + 128)
        rows = main_v[:, :, lanes].reshape(SPAN, 128).astype(F32)
        rim = rim_v[:, lanes].astype(F32)[8:16, :]
        conv_v[:, lanes] = conv(rim, rows, taps_v[:, lanes]).astype(BF16)

    scaled = (conv_v[...].astype(F32) * tail_x[...]).astype(BF16)
    local = jnp.dot(key_t, scaled, preferred_element_type=F32).astype(BF16)
    for r in range(4):
        st_send[r, 0:32, :] = local[32 * r : 32 * r + 32, :]
        st_send[r, 32:40, :] = gate_rows

    def state_piece(c):
        return st_send.at[lax.rem(c, 4), :, pl.ds(pl.multiple_of(128 * lax.div(c, 4), 128), 128)]

    def send_state(d, carry):
        c = peer(d)
        remote(state_piece(c), st_recv.at[me], st_ss, st_rs, {"ctx": c}).start()
        return carry

    pltpu.make_async_copy(state_piece(me), st_recv.at[me], st_rs).start()
    lax.fori_loop(1, NC, send_state, 0)

    def second_g(half):
        def one(d, carry):
            o = peer(d)
            for k in range(BPD):
                send_g[half, BPD * o + k] = recv_g[inv[0, BPD * o + k], half]
            src = send_g.at[half, owner_slots(o)]
            target = gate_piece(main_g, me, half)
            remote(src, target, g2_send.at[half], g2_recv.at[half], {"ctx": o}).start()
            return carry

        lax.fori_loop(1, NC, one, 0)
        for k in range(BPD):
            send_g[half, BPD * me + k] = recv_g[inv[0, BPD * me + k], half]
        src = send_g.at[half, owner_slots(me)]
        pltpu.make_async_copy(src, gate_piece(main_g, me, half), g2_recv.at[half]).start()

    left = iota((SPAN, 128), 1) < 64

    def intra(g):
        lanes = slice(128 * g, 128 * g + 128)
        pair = conv_v[:, lanes]
        found = []
        for h in (2 * g, 2 * g + 1):
            decay = jnp.exp(jnp.minimum(sums[:, h : h + 1] - sums_t[h : h + 1, :], 0.0))
            mix = (decay * (product[...] * step_t[h : h + 1, :])).astype(BF16)
            found.append(jnp.dot(mix, pair, preferred_element_type=F32))
        gain = jnp.where(left, skip[0, 2 * g], skip[0, 2 * g + 1])
        mixed = jnp.where(left, found[0], found[1]) + gain * pair.astype(F32)
        y[:, :, :, lanes] = mixed.reshape(8, 2, 16, 128)

    for g in range(3):
        intra(g)

    pltpu.make_async_copy(recv_g, recv_g, g_recv).wait()
    second_g(0)

    for g in range(3, 6):
        intra(g)

    pltpu.make_async_copy(st_recv, st_recv, st_rs).wait()
    state = jnp.zeros((32, 128), F32)
    for o in range(NC):
        ent_send[o] = state.astype(BF16)
        part = st_recv[o, 0:32, :].astype(F32)
        pair = st_recv[o, 32:40, :].astype(F32)
        state = (pair[0:1, :] + pair[1:2, :]) * state + part

    def ent_target():
        return ent.at[pl.ds(pl.multiple_of(32 * lax.rem(me, 4), 32), 32), pl.ds(pl.multiple_of(128 * lax.div(me, 4), 128), 128)]

    def send_ent(d, carry):
        o = peer(d)
        remote(ent_send.at[o], ent_target(), en_ss, en_rs, {"ctx": o}).start()
        return carry

    pltpu.make_async_copy(ent_send.at[me], ent_target(), en_rs).start()
    lax.fori_loop(1, NC, send_ent, 0)

    second_g(1)

    for g in range(6, 8):
        intra(g)

    pltpu.make_async_copy(ent, ent, en_rs).wait()
    for g in range(8):
        lanes = slice(128 * g, 128 * g + 128)
        carried = jnp.dot(conv_q[...], ent[:, lanes], preferred_element_type=F32)
        carried = inflow_x[:, lanes] * carried
        y[:, :, :, lanes] = y[:, :, :, lanes] + carried.reshape(8, 2, 16, 128)

    def s1_copy(half, i):
        return remote(
            s1_send.at[half, i], s1_recv.at[half, i], s1_ss.at[half, i], s1_rs.at[half, i], {"tp": sibling}
        )

    def s2_copy(half, i, dx):
        return remote(
            s2_send.at[half, i, dx - 1],
            s2_recv.at[half, i, 3 - dx],
            s2_ss.at[half, i, dx - 1],
            s2_rs.at[half, i, 3 - dx],
            {"tp": lax.rem(my_x + dx, 4) * 2 + core},
        )

    for half in range(2):
        wait_g = main_g.at[:, :, half]
        pltpu.make_async_copy(wait_g, wait_g, g2_recv.at[half]).wait()
        squares = jnp.zeros((128, 128), F32)
        gated = []
        for g in range(8):
            lanes = slice(128 * g, 128 * g + 128)
            gate = main_g[:, :, half, :, :, lanes].reshape(128, 128).astype(F32)
            found = y[:, half, :, lanes].reshape(128, 128) * silu(gate)
            squares = squares + found * found
            gated.append(found)
        mean = jnp.sum(squares, axis=1, keepdims=True) * (1.0 / WIDTH)
        scale = lax.rsqrt(mean + 1e-05)
        for g in range(8):
            lanes = slice(128 * g, 128 * g + 128)
            normed[half, :, lanes] = (gated[g] * scale * norm_gain[:, lanes]).astype(BF16)
        if half == 0:
            weight_copy.wait()
        for i in range(NCHUNK + 1):
            if i < NCHUNK:
                part = jnp.dot(
                    normed[half], weight[:, CW * i : CW * i + CW], preferred_element_type=F32
                )
                own_part[...] = part.reshape(4, 2, 16, CW)
                s1_send[half, i] = own_part[:, 1 - core].astype(BF16)
                s1_copy(half, i).start()
                keep[half, i] = own_part[:, core]
            if i > 0:
                k = i - 1
                s1_copy(half, k).wait_recv()
                keep[half, k] = keep[half, k] + s1_recv[half, k].astype(F32)
                for dx in (2, 1, 3):
                    s2_send[half, k, dx - 1] = keep[half, k, lax.rem(my_x + dx, 4)].astype(BF16)
                    s2_copy(half, k, dx).start()

    for half in range(2):
        for i in range(NCHUNK):
            both = keep[half, i, my_x]
            for dx in range(1, 4):
                s2_copy(half, i, dx).wait_recv()
                both = both + s2_recv[half, i, 3 - dx].astype(F32)
            out[16 * half : 16 * half + 16, CW * i : CW * i + CW] = both.astype(BF16)

    most = pl.ds(0, BPD * (NC - 1))
    for ref, sem in ((recv_v, v_send), (recv_g, g_send), (send_v, v2_send)):
        pltpu.make_async_copy(ref.at[most], ref.at[most], sem).wait()

    @pl.when(me < 24)
    def _():
        some = recv_s.at[pl.ds(0, BPD * 23)]
        pltpu.make_async_copy(some, some, k_send).wait()
        some = send_s.at[most]
        pltpu.make_async_copy(some, some, k2_send).wait()

    @pl.when(me >= 24)
    def _():
        some = recv_s.at[pl.ds(0, BPD * 24)]
        pltpu.make_async_copy(some, some, k_send).wait()

    @pl.when(v_rim)
    def _():
        some = rim_send_v.at[pl.ds(0, NC - 1)]
        pltpu.make_async_copy(some, some, rv_send).wait()

    @pl.when((lax.rem(me, 8) == 7) & (me < 16))
    def _():
        some = rim_send_s.at[pl.ds(0, NC - 1)]
        pltpu.make_async_copy(some, some, rk_send).wait()

    for half in range(2):
        some = send_g.at[half, most]
        pltpu.make_async_copy(some, some, g2_send.at[half]).wait()
    some = st_recv.at[pl.ds(0, NC - 1)]
    pltpu.make_async_copy(some, some, st_ss).wait()
    some = ent_send.at[pl.ds(0, NC - 1)]
    pltpu.make_async_copy(some, some, en_ss).wait()
    for i in range(NCHUNK):
        for half in range(2):
            s1_copy(half, i).wait_send()
            for dx in range(1, 4):
                s2_copy(half, i, dx).wait_send()


def on_device(
    values_in,
    gate_in,
    keys_in,
    queries_in,
    step_in,
    block_order,
    doc_lengths,
    conv_values,
    conv_keys,
    conv_queries,
    decay_log,
    step_bias,
    skip_gain,
    norm_gain,
    out_weight,
):
    count = NC * BPD
    vmem = pl.BlockSpec(memory_space=pltpu.VMEM)
    hbm = pl.BlockSpec(memory_space=pltpu.HBM)
    dma = pltpu.SemaphoreType.DMA
    scratch = [
        pltpu.VMEM((1, count), jnp.int32),
        pltpu.SMEM((1, DOCS), jnp.int32),
        pltpu.SMEM((1, HEADS), F32),
        pltpu.VMEM((HEADS, SPAN), BF16),
        pltpu.VMEM((4, WIDTH), F32),
        pltpu.VMEM((4, STATE), F32),
        pltpu.VMEM((4, STATE), F32),
        pltpu.VMEM((1, HEADS), F32),
        pltpu.VMEM((1, HEADS), F32),
        pltpu.VMEM((1, WIDTH), F32),
        pltpu.VMEM((1, count), jnp.int32),
        pltpu.SMEM((1, count), jnp.int32),
        dma((10,)),
        dma(()),
        pltpu.VMEM((WIDTH, OUTW), BF16),
        pltpu.VMEM((BPD, BLK, 128), BF16),
        pltpu.VMEM((8, 128), F32),
        pltpu.VMEM((count, 16, 128), BF16),
        pltpu.VMEM((count, 2, 8, 128), BF16),
        pltpu.VMEM((count, 8, 128), BF16),
        pltpu.VMEM((count, 16, 128), BF16),
        pltpu.VMEM((2, count, 8, 128), BF16),
        pltpu.VMEM((count, 8, 128), BF16),
        pltpu.VMEM((BPD, BLK, WIDTH), BF16),
        pltpu.VMEM((BPD, 2, 2, 2, 8, WIDTH), BF16),
        pltpu.VMEM((3, BPD, BLK, 128), BF16),
        pltpu.VMEM((16, WIDTH), BF16),
        pltpu.VMEM((2, 8, 128), BF16),
        pltpu.VMEM((NC, 16, 128), BF16),
        pltpu.VMEM((NC, 8, 128), BF16),
        pltpu.VMEM((SPAN, WIDTH), BF16),
        pltpu.VMEM((SPAN, STATE), BF16),
        pltpu.VMEM((SPAN, STATE), BF16),
        pltpu.VMEM((3, SPAN, 128), F32),
        pltpu.VMEM((SPAN, SPAN), F32),
        pltpu.VMEM((SPAN, WIDTH), F32),
        pltpu.VMEM((SPAN, WIDTH), F32),
        pltpu.VMEM((4, 40, WIDTH), BF16),
        pltpu.VMEM((NC, 40, 128), BF16),
        pltpu.VMEM((NC, 32, 128), BF16),
        pltpu.VMEM((STATE, WIDTH), BF16),
        pltpu.VMEM((8, 2, 16, WIDTH), F32),
        pltpu.VMEM((2, 128, WIDTH), BF16),
        pltpu.VMEM((2, NCHUNK, 4, 16, CW), BF16),
        pltpu.VMEM((2, NCHUNK, 4, 16, CW), BF16),
        pltpu.VMEM((4, 2, 16, CW), F32),
        pltpu.VMEM((2, NCHUNK, 4, 16, CW), F32),
        pltpu.VMEM((2, NCHUNK, 3, 16, CW), BF16),
        pltpu.VMEM((2, NCHUNK, 3, 16, CW), BF16),
        dma(()),
    ]
    scratch += [dma(()) for _ in range(6)] + [dma(()), dma(())] + [dma((2,)), dma((2,))]
    scratch += [dma(()) for _ in range(6)]
    scratch += [dma(()) for _ in range(4)]
    scratch += [dma((2, NCHUNK)), dma((2, NCHUNK)), dma((2, NCHUNK, 3)), dma((2, NCHUNK, 3))]
    call = pl.pallas_call(
        body,
        out_shape=jax.ShapeDtypeStruct((SPAN // 8, OUTW), BF16),
        in_specs=[hbm] * 15,
        out_specs=vmem,
        scratch_shapes=scratch,
        compiler_params=pltpu.CompilerParams(
            collective_id=0, has_side_effects=True, vmem_limit_bytes=60 << 20
        ),
        name="layer",
    )
    return call(
        block_order.reshape(1, count),
        doc_lengths.reshape(1, DOCS),
        skip_gain.reshape(1, HEADS),
        values_in.reshape(BPD, BLK, WIDTH),
        gate_in.reshape(BPD, 2, 2, 2, 8, WIDTH),
        keys_in.reshape(BPD, BLK, STATE),
        queries_in.reshape(BPD, BLK, STATE),
        step_in.T,
        conv_values,
        conv_keys,
        conv_queries,
        decay_log.reshape(1, HEADS),
        step_bias.reshape(1, HEADS),
        norm_gain.reshape(1, WIDTH),
        out_weight,
    )


def solution(mesh):
    in_specs = (
        P("ctx", "tp"),
        P("ctx", "tp"),
        P("ctx", "tp"),
        P("ctx", "tp"),
        P("ctx", "tp"),
        P(),
        P(),
        P(None, "tp"),
        P(None, "tp"),
        P(None, "tp"),
        P("tp"),
        P("tp"),
        P("tp"),
        P("tp"),
        P("tp", None),
    )
    out_specs = P(("ctx", "tp"), None)
    return jax.shard_map(
        on_device, mesh=mesh, in_specs=in_specs, out_specs=out_specs, check_vma=False
    )
```

```python
import functools

import jax
import jax.numpy as jnp
from jax import lax
from jax.experimental import pallas as pl
from jax.experimental.pallas import tpu as pltpu
from jax.sharding import PartitionSpec as P

NC = 32
BPD = 4
BLK = 64
SPAN = 256
WIDTH = 1024
HEADS = 16
STATE = 128
OUTW = 4096
DOCS = 16
NCHUNK = 4
CW = OUTW // NCHUNK
FIRST_G = 12
MESH = pl.DeviceIdType.MESH
F32 = jnp.float32
BF16 = jnp.bfloat16
HIGHEST = lax.Precision.HIGHEST


def silu(x):
    return x * jax.nn.sigmoid(x)


def iota(shape, axis):
    return lax.broadcasted_iota(jnp.int32, shape, axis)


def body(
    order_hbm,
    lengths_hbm,
    skip_hbm,
    values,
    gates,
    keys,
    queries,
    steps_hbm,
    taps_v_hbm,
    taps_k_hbm,
    taps_q_hbm,
    decay_hbm,
    bias_hbm,
    gain_hbm,
    weight_hbm,
    out,
    order,
    doc_lengths,
    skip,
    steps_in,
    taps_v,
    taps_k,
    taps_q,
    decay_log,
    step_bias,
    norm_gain,
    inv_row,
    inv,
    local_sem,
    inv_sem,
    weight,
    step_pad,
    rows16,
    recv_v,
    recv_g,
    recv_s,
    send_v,
    send_g,
    send_s,
    main_v,
    main_g,
    main_s,
    main_step,
    rim_v,
    rim_s,
    rim_send_v,
    rim_send_s,
    conv_v,
    conv_k,
    conv_q,
    masks,
    product,
    tail_x,
    inflow_x,
    st_send,
    st_recv,
    ent_send,
    ent,
    y,
    normed,
    s1_send,
    s1_recv,
    own_part,
    keep,
    s2_send,
    s2_recv,
    w_sem,
    v_send,
    v_recv,
    g_send,
    g_recv,
    k_send,
    k_recv,
    v2_send,
    v2_recv,
    g2_send,
    g2_recv,
    k2_send,
    k2_recv,
    rv_send,
    rv_recv,
    rk_send,
    rk_recv,
    st_ss,
    st_rs,
    en_ss,
    en_rs,
    s1_ss,
    s1_rs,
    s2_ss,
    s2_rs,
    sp_recv,
):
    me = lax.axis_index("ctx")
    tp = lax.axis_index("tp")
    my_x = lax.div(tp, 2)
    core = lax.rem(tp, 2)
    sibling = my_x * 2 + (1 - core)

    loads = [
        pltpu.make_async_copy(src, dst, local_sem.at[i])
        for i, (src, dst) in enumerate(
            (
                (steps_hbm, steps_in),
                (order_hbm, order),
                (lengths_hbm, doc_lengths),
                (skip_hbm, skip),
                (taps_v_hbm, taps_v),
                (taps_k_hbm, taps_k),
                (taps_q_hbm, taps_q),
                (decay_hbm, decay_log),
                (bias_hbm, step_bias),
                (gain_hbm, norm_gain),
            )
        )
    ]
    barrier = pltpu.get_barrier_semaphore()

    def peer(d):
        return lax.rem(me + d, NC)

    def greet(d, carry):
        pl.semaphore_signal(barrier, inc=1, device_id={"ctx": peer(d)}, device_id_type=MESH)
        return carry

    lax.fori_loop(1, NC, greet, 0)
    pl.semaphore_signal(barrier, inc=1, device_id={"tp": sibling}, device_id_type=MESH)
    for dx in range(1, 4):
        other = lax.rem(my_x + dx, 4) * 2 + core
        pl.semaphore_signal(barrier, inc=1, device_id={"tp": other}, device_id_type=MESH)

    for load in loads:
        load.start()
    weight_copy = pltpu.make_async_copy(weight_hbm, weight, w_sem)
    weight_copy.start()
    for load in loads:
        load.wait()
    wide = jnp.concatenate(
        [steps_in[...].astype(F32), jnp.zeros((128 - HEADS, SPAN), F32)], axis=0
    )
    by_token = jnp.transpose(wide)
    for b in range(BPD):
        tile = by_token[BLK * b : BLK * b + 8, :]
        for a in range(1, 8):
            first = BLK * b + 8 * a
            tile = tile + pltpu.roll(by_token[first : first + 8, :], HEADS * a, 1)
        step_pad[b] = tile.astype(BF16)
    rows16[...] = jnp.zeros_like(rows16)
    rows16[0:1, 0:HEADS] = step_bias[...]
    rows16[1:2, 0:HEADS] = decay_log[...]
    side = (NC * BPD, NC * BPD)
    placed = jnp.transpose(jnp.broadcast_to(order[...], side))
    found_at = jnp.where(placed == iota(side, 1), iota(side, 0), 0)
    inv_row[0:1, :] = jnp.max(found_at, axis=0, keepdims=True)
    inv_copy = pltpu.make_async_copy(inv_row, inv, inv_sem)
    inv_copy.start()

    pl.semaphore_wait(barrier, NC - 1 + 4)

    def remote(src, dst, ss, rs, where):
        return pltpu.make_async_remote_copy(
            src_ref=src, dst_ref=dst, send_sem=ss, recv_sem=rs, device_id=where, device_id_type=MESH
        )

    def piece(ref, c):
        return ref.at[:, pl.ds(pl.multiple_of(16 * lax.rem(c, 4), 16), 16), pl.ds(pl.multiple_of(128 * lax.div(c, 4), 128), 128)]

    def octet(ref, c):
        return ref.at[:, pl.ds(pl.multiple_of(8 * lax.rem(c, 8), 8), 8), :]

    my_slots = pl.ds(BPD * me, BPD)

    def gate_piece(ref, c, half):
        turn = lax.rem(c, 4)
        lanes = pl.ds(pl.multiple_of(128 * lax.div(c, 4), 128), 128)
        return ref.at[:, lax.div(turn, 2), half, lax.rem(turn, 2), :, lanes]


    def small_source(c, act):
        @pl.when(c < 8)
        def _():
            act(octet(keys, c))

        @pl.when((c >= 8) & (c < 16))
        def _():
            act(octet(queries, c))

    def first_v(d, carry):
        c = peer(d)
        where = {"ctx": c}
        small_source(c, lambda src: remote(src, recv_s.at[my_slots], k_send, k_recv, where).start())
        remote(piece(values, c), recv_v.at[my_slots], v_send, v_recv, where).start()
        return carry

    lax.fori_loop(1, NC, first_v, 0)
    small_source(me, lambda src: pltpu.make_async_copy(src, recv_s.at[my_slots], k_recv).start())
    pltpu.make_async_copy(piece(values, me), recv_v.at[my_slots], v_recv).start()

    holder = 16

    @pl.when(me != holder)
    def _():
        remote(step_pad, recv_s.at[my_slots], k_send, k_recv, {"ctx": holder}).start()

    @pl.when(me == holder)
    def _():
        pltpu.make_async_copy(step_pad, recv_s.at[my_slots], k_recv).start()

    def first_g(d, carry):
        c = peer(d)
        remote(gate_piece(gates, c, slice(None)), recv_g.at[my_slots], g_send, g_recv, {"ctx": c}).start()
        return carry

    lax.fori_loop(1, FIRST_G, first_g, 0)
    inv_copy.wait()

    starts = []
    total = jnp.int32(0)
    for k in range(DOCS):
        starts.append(total - me * SPAN)
        total = total + doc_lengths[0, k]

    row = iota((SPAN, 128), 0)

    def opening_at(position):
        hit = position == starts[0]
        for k in range(1, DOCS):
            hit = hit | (position == starts[k])
        return hit

    open0 = opening_at(row)
    open1 = opening_at(row - 1)
    open2 = opening_at(row - 2)
    masks[0] = jnp.where(open0 | open1 | open2, 0.0, 1.0).astype(F32)
    masks[1] = jnp.where(open0 | open1, 0.0, 1.0).astype(F32)
    masks[2] = jnp.where(open0, 0.0, 1.0).astype(F32)

    tail_cut = jnp.zeros((SPAN, 128), jnp.int32)
    head_cut = jnp.zeros((SPAN, 128), jnp.int32)
    for k in range(DOCS):
        inside = (row * 0 + starts[k] >= 0) & (row * 0 + starts[k] < SPAN)
        tail_cut = tail_cut | jnp.where(inside & (row < starts[k]), 1, 0)
        head_cut = head_cut | jnp.where(inside & (row >= starts[k]), 1, 0)

    def owner_slots(o):
        return pl.ds(BPD * o, BPD)

    def fill(src, dst, o):
        for k in range(BPD):
            dst[BPD * o + k] = src[inv[0, BPD * o + k]]

    def before(o):
        return inv[0, lax.rem(BPD * o + NC * BPD - 1, NC * BPD)]

    has_small = me < holder
    kind = lax.div(me, 8)

    def small_target(i):
        return main_s.at[i, :, pl.ds(pl.multiple_of(8 * lax.rem(me, 8), 8), 8), :]

    @pl.when(has_small)
    def _():
        pltpu.make_async_copy(recv_s, recv_s, k_recv).wait()
        sends_rim = (lax.rem(me, 8) == 7) & (me < 16)

        def second_s(d, carry):
            o = peer(d)
            where = {"ctx": o}
            fill(recv_s, send_s, o)
            remote(send_s.at[owner_slots(o)], small_target(kind), k2_send, k2_recv, where).start()

            @pl.when(sends_rim)
            def _():
                rim_send_s[o] = recv_s[before(o)]
                remote(rim_send_s.at[o], rim_s.at[kind], rk_send, rk_recv, where).start()

            return carry

        lax.fori_loop(1, NC, second_s, 0)
        fill(recv_s, send_s, me)
        pltpu.make_async_copy(send_s.at[owner_slots(me)], small_target(kind), k2_recv).start()

        @pl.when(sends_rim)
        def _():
            rim_send_s[me] = recv_s[before(me)]
            pltpu.make_async_copy(rim_send_s.at[me], rim_s.at[kind], rk_recv).start()

    @pl.when(me == holder)
    def _():
        pltpu.make_async_copy(recv_s, recv_s, k_recv).wait()

        def second_step(d, carry):
            o = peer(d)
            fill(recv_s, send_s, o)
            remote(send_s.at[owner_slots(o)], main_step, k2_send, sp_recv, {"ctx": o}).start()
            return carry

        lax.fori_loop(1, NC, second_step, 0)
        fill(recv_s, send_s, me)
        pltpu.make_async_copy(send_s.at[owner_slots(me)], main_step, sp_recv).start()

    pltpu.make_async_copy(recv_v, recv_v, v_recv).wait()
    v_rim = lax.rem(me, 4) == 3

    def rim_target():
        return rim_v.at[:, pl.ds(pl.multiple_of(128 * lax.div(me, 4), 128), 128)]

    def second_v(d, carry):
        o = peer(d)
        where = {"ctx": o}
        fill(recv_v, send_v, o)
        remote(send_v.at[owner_slots(o)], piece(main_v, me), v2_send, v2_recv, where).start()

        @pl.when(v_rim)
        def _():
            rim_send_v[o] = recv_v[before(o)]
            remote(rim_send_v.at[o], rim_target(), rv_send, rv_recv, where).start()

        return carry

    lax.fori_loop(1, NC, second_v, 0)
    fill(recv_v, send_v, me)
    pltpu.make_async_copy(send_v.at[owner_slots(me)], piece(main_v, me), v2_recv).start()

    @pl.when(v_rim)
    def _():
        rim_send_v[me] = recv_v[before(me)]
        pltpu.make_async_copy(rim_send_v.at[me], rim_target(), rv_recv).start()

    lax.fori_loop(FIRST_G, NC, first_g, 0)
    pltpu.make_async_copy(gate_piece(gates, me, slice(None)), recv_g.at[my_slots], g_recv).start()

    pltpu.make_async_copy(main_s, main_s, k2_recv).wait()
    pltpu.make_async_copy(rim_s, rim_s, rk_recv).wait()
    pltpu.make_async_copy(main_step, main_step, sp_recv).wait()

    def conv(rim, rows, taps):
        ext = jnp.concatenate([rim, rows], axis=0)
        acc = (masks[0] * taps[0:1, :]) * pltpu.roll(ext, 3, 0)[8:, :]
        acc = acc + (masks[1] * taps[1:2, :]) * pltpu.roll(ext, 2, 0)[8:, :]
        acc = acc + (masks[2] * taps[2:3, :]) * pltpu.roll(ext, 1, 0)[8:, :]
        acc = acc + taps[3:4, :] * rows
        return silu(acc)

    key_f = conv(rim_s[0].astype(F32), main_s[0].reshape(SPAN, 128).astype(F32), taps_k)
    query_f = conv(rim_s[1].astype(F32), main_s[1].reshape(SPAN, 128).astype(F32), taps_q)
    conv_k[...] = key_f.astype(BF16)
    conv_q[...] = query_f.astype(BF16)

    unpacked = []
    for b in range(BPD):
        tile = main_step[b].astype(F32)
        unpacked.append(tile)
        for a in range(1, 8):
            unpacked.append(pltpu.roll(tile, 128 - HEADS * a, 1))
    pre = jnp.concatenate(unpacked, axis=0)
    pre = jnp.where(iota((SPAN, 128), 1) < HEADS, pre, 0.0) + rows16[0:1, :]
    small = jnp.exp(-jnp.abs(pre))
    one_more = 1.0 + small
    gap = one_more - 1.0
    log1p = jnp.where(gap == 0.0, small, jnp.log(one_more) * small / jnp.where(gap == 0.0, 1.0, gap))
    step = jnp.maximum(pre, 0.0) + log1p
    sums = -jnp.exp(rows16[1:2, :]) * step
    for k in (1, 2, 4, 8, 16, 32, 64, 128):
        sums = sums + jnp.where(row >= k, pltpu.roll(sums, k, 0), 0.0)
    last = sums[SPAN - 1 : SPAN, :]
    tail = jnp.where(tail_cut > 0, 0.0, jnp.exp(last - sums) * step)
    inflow = jnp.where(head_cut > 0, 0.0, jnp.exp(sums))
    spread = jnp.where(
        lax.div(iota((128, WIDTH), 1), 64) == iota((128, WIDTH), 0), 1.0, 0.0
    ).astype(F32)
    tail_x[...] = jnp.dot(tail, spread, precision=HIGHEST, preferred_element_type=F32)
    inflow_x[...] = jnp.dot(inflow, spread, precision=HIGHEST, preferred_element_type=F32)
    gate_row = inflow_x[SPAN - 1 : SPAN, :]
    gate_hi = gate_row.astype(BF16)
    gate_lo = (gate_row - gate_hi.astype(F32)).astype(BF16)
    which = iota((8, WIDTH), 0)
    gate_rows = jnp.where(
        which == 0, gate_hi.astype(F32), jnp.where(which == 1, gate_lo.astype(F32), 0.0)
    ).astype(BF16)
    sums_t = jnp.transpose(sums)
    step_t = jnp.transpose(step)
    key_t = jnp.transpose(conv_k[...].astype(F32)).astype(BF16)
    t_id = iota((SPAN, SPAN), 0)
    u_id = iota((SPAN, SPAN), 1)
    drop = u_id > t_id
    for k in range(DOCS):
        drop = drop | ((u_id < starts[k]) & (t_id >= starts[k]))
    inner = lax.dot_general(
        conv_q[...], conv_k[...], (((1,), (1,)), ((), ())), preferred_element_type=F32
    )
    product[...] = jnp.where(drop, 0.0, inner)

    pltpu.make_async_copy(main_v, main_v, v2_recv).wait()
    pltpu.make_async_copy(rim_v, rim_v, rv_recv).wait()
    for g in range(8):
        lanes = slice(128 * g, 128 * g + 128)
        rows = main_v[:, :, lanes].reshape(SPAN, 128).astype(F32)
        rim = rim_v[:, lanes].astype(F32)[8:16, :]
        conv_v[:, lanes] = conv(rim, rows, taps_v[:, lanes]).astype(BF16)

    scaled = (conv_v[...].astype(F32) * tail_x[...]).astype(BF16)
    local = jnp.dot(key_t, scaled, preferred_element_type=F32).astype(BF16)
    for r in range(4):
        st_send[r, 0:32, :] = local[32 * r : 32 * r + 32, :]
        st_send[r, 32:40, :] = gate_rows

    def state_piece(c):
        return st_send.at[lax.rem(c, 4), :, pl.ds(pl.multiple_of(128 * lax.div(c, 4), 128), 128)]

    def send_state(d, carry):
        c = peer(d)
        remote(state_piece(c), st_recv.at[me], st_ss, st_rs, {"ctx": c}).start()
        return carry

    pltpu.make_async_copy(state_piece(me), st_recv.at[me], st_rs).start()
    lax.fori_loop(1, NC, send_state, 0)

    def second_g(half):
        def one(d, carry):
            o = peer(d)
            for k in range(BPD):
                send_g[half, BPD * o + k] = recv_g[inv[0, BPD * o + k], half]
            src = send_g.at[half, owner_slots(o)]
            target = gate_piece(main_g, me, half)
            remote(src, target, g2_send.at[half], g2_recv.at[half], {"ctx": o}).start()
            return carry

        lax.fori_loop(1, NC, one, 0)
        for k in range(BPD):
            send_g[half, BPD * me + k] = recv_g[inv[0, BPD * me + k], half]
        src = send_g.at[half, owner_slots(me)]
        pltpu.make_async_copy(src, gate_piece(main_g, me, half), g2_recv.at[half]).start()

    left = iota((SPAN, 128), 1) < 64

    def intra(g):
        lanes = slice(128 * g, 128 * g + 128)
        pair = conv_v[:, lanes]
        found = []
        for h in (2 * g, 2 * g + 1):
            decay = jnp.exp(jnp.minimum(sums[:, h : h + 1] - sums_t[h : h + 1, :], 0.0))
            mix = (decay * (product[...] * step_t[h : h + 1, :])).astype(BF16)
            found.append(jnp.dot(mix, pair, preferred_element_type=F32))
        gain = jnp.where(left, skip[0, 2 * g], skip[0, 2 * g + 1])
        mixed = jnp.where(left, found[0], found[1]) + gain * pair.astype(F32)
        y[:, :, :, lanes] = mixed.reshape(8, 2, 16, 128)

    for g in range(3):
        intra(g)

    pltpu.make_async_copy(recv_g, recv_g, g_recv).wait()
    second_g(0)

    for g in range(3, 6):
        intra(g)

    pltpu.make_async_copy(st_recv, st_recv, st_rs).wait()
    state = jnp.zeros((32, 128), F32)
    for o in range(NC):
        ent_send[o] = state.astype(BF16)
        part = st_recv[o, 0:32, :].astype(F32)
        pair = st_recv[o, 32:40, :].astype(F32)
        state = (pair[0:1, :] + pair[1:2, :]) * state + part

    def ent_target():
        return ent.at[pl.ds(pl.multiple_of(32 * lax.rem(me, 4), 32), 32), pl.ds(pl.multiple_of(128 * lax.div(me, 4), 128), 128)]

    def send_ent(d, carry):
        o = peer(d)
        remote(ent_send.at[o], ent_target(), en_ss, en_rs, {"ctx": o}).start()
        return carry

    pltpu.make_async_copy(ent_send.at[me], ent_target(), en_rs).start()
    lax.fori_loop(1, NC, send_ent, 0)

    second_g(1)

    for g in range(6, 8):
        intra(g)

    pltpu.make_async_copy(ent, ent, en_rs).wait()
    for g in range(8):
        lanes = slice(128 * g, 128 * g + 128)
        carried = jnp.dot(conv_q[...], ent[:, lanes], preferred_element_type=F32)
        carried = inflow_x[:, lanes] * carried
        y[:, :, :, lanes] = y[:, :, :, lanes] + carried.reshape(8, 2, 16, 128)

    def s1_copy(half, i):
        return remote(
            s1_send.at[half, i], s1_recv.at[half, i], s1_ss.at[half, i], s1_rs.at[half, i], {"tp": sibling}
        )

    def s2_copy(half, i, dx):
        return remote(
            s2_send.at[half, i, dx - 1],
            s2_recv.at[half, i, 3 - dx],
            s2_ss.at[half, i, dx - 1],
            s2_rs.at[half, i, 3 - dx],
            {"tp": lax.rem(my_x + dx, 4) * 2 + core},
        )

    for half in range(2):
        wait_g = main_g.at[:, :, half]
        pltpu.make_async_copy(wait_g, wait_g, g2_recv.at[half]).wait()
        squares = jnp.zeros((128, 128), F32)
        gated = []
        for g in range(8):
            lanes = slice(128 * g, 128 * g + 128)
            gate = main_g[:, :, half, :, :, lanes].reshape(128, 128).astype(F32)
            found = y[:, half, :, lanes].reshape(128, 128) * silu(gate)
            squares = squares + found * found
            gated.append(found)
        mean = jnp.sum(squares, axis=1, keepdims=True) * (1.0 / WIDTH)
        scale = lax.rsqrt(mean + 1e-05)
        for g in range(8):
            lanes = slice(128 * g, 128 * g + 128)
            normed[half, :, lanes] = (gated[g] * scale * norm_gain[:, lanes]).astype(BF16)
        if half == 0:
            weight_copy.wait()
        for i in range(NCHUNK + 1):
            if i < NCHUNK:
                part = jnp.dot(
                    normed[half], weight[:, CW * i : CW * i + CW], preferred_element_type=F32
                )
                own_part[...] = part.reshape(4, 2, 16, CW)
                s1_send[half, i] = own_part[:, 1 - core].astype(BF16)
                s1_copy(half, i).start()
                keep[half, i] = own_part[:, core]
            if i > 0:
                k = i - 1
                s1_copy(half, k).wait_recv()
                keep[half, k] = keep[half, k] + s1_recv[half, k].astype(F32)
                for dx in (2, 1, 3):
                    s2_send[half, k, dx - 1] = keep[half, k, lax.rem(my_x + dx, 4)].astype(BF16)
                    s2_copy(half, k, dx).start()

    for half in range(2):
        for i in range(NCHUNK):
            both = keep[half, i, my_x]
            for dx in range(1, 4):
                s2_copy(half, i, dx).wait_recv()
                both = both + s2_recv[half, i, 3 - dx].astype(F32)
            out[16 * half : 16 * half + 16, CW * i : CW * i + CW] = both.astype(BF16)

    most = pl.ds(0, BPD * (NC - 1))
    for ref, sem in ((recv_v, v_send), (recv_g, g_send), (send_v, v2_send)):
        pltpu.make_async_copy(ref.at[most], ref.at[most], sem).wait()

    @pl.when(me <= holder)
    def _():
        some = recv_s.at[pl.ds(0, BPD * 16)]
        pltpu.make_async_copy(some, some, k_send).wait()
        some = send_s.at[most]
        pltpu.make_async_copy(some, some, k2_send).wait()

    @pl.when(me > holder)
    def _():
        some = recv_s.at[pl.ds(0, BPD * 17)]
        pltpu.make_async_copy(some, some, k_send).wait()

    @pl.when(v_rim)
    def _():
        some = rim_send_v.at[pl.ds(0, NC - 1)]
        pltpu.make_async_copy(some, some, rv_send).wait()

    @pl.when((lax.rem(me, 8) == 7) & (me < 16))
    def _():
        some = rim_send_s.at[pl.ds(0, NC - 1)]
        pltpu.make_async_copy(some, some, rk_send).wait()

    for half in range(2):
        some = send_g.at[half, most]
        pltpu.make_async_copy(some, some, g2_send.at[half]).wait()
    some = st_recv.at[pl.ds(0, NC - 1)]
    pltpu.make_async_copy(some, some, st_ss).wait()
    some = ent_send.at[pl.ds(0, NC - 1)]
    pltpu.make_async_copy(some, some, en_ss).wait()
    for i in range(NCHUNK):
        for half in range(2):
            s1_copy(half, i).wait_send()
            for dx in range(1, 4):
                s2_copy(half, i, dx).wait_send()


def on_device(
    values_in,
    gate_in,
    keys_in,
    queries_in,
    step_in,
    block_order,
    doc_lengths,
    conv_values,
    conv_keys,
    conv_queries,
    decay_log,
    step_bias,
    skip_gain,
    norm_gain,
    out_weight,
):
    count = NC * BPD
    vmem = pl.BlockSpec(memory_space=pltpu.VMEM)
    hbm = pl.BlockSpec(memory_space=pltpu.HBM)
    dma = pltpu.SemaphoreType.DMA
    scratch = [
        pltpu.VMEM((1, count), jnp.int32),
        pltpu.SMEM((1, DOCS), jnp.int32),
        pltpu.SMEM((1, HEADS), F32),
        pltpu.VMEM((HEADS, SPAN), BF16),
        pltpu.VMEM((4, WIDTH), F32),
        pltpu.VMEM((4, STATE), F32),
        pltpu.VMEM((4, STATE), F32),
        pltpu.VMEM((1, HEADS), F32),
        pltpu.VMEM((1, HEADS), F32),
        pltpu.VMEM((1, WIDTH), F32),
        pltpu.VMEM((1, count), jnp.int32),
        pltpu.SMEM((1, count), jnp.int32),
        dma((10,)),
        dma(()),
        pltpu.VMEM((WIDTH, OUTW), BF16),
        pltpu.VMEM((BPD, 8, 128), BF16),
        pltpu.VMEM((8, 128), F32),
        pltpu.VMEM((count, 16, 128), BF16),
        pltpu.VMEM((count, 2, 8, 128), BF16),
        pltpu.VMEM((count, 8, 128), BF16),
        pltpu.VMEM((count, 16, 128), BF16),
        pltpu.VMEM((2, count, 8, 128), BF16),
        pltpu.VMEM((count, 8, 128), BF16),
        pltpu.VMEM((BPD, BLK, WIDTH), BF16),
        pltpu.VMEM((BPD, 2, 2, 2, 8, WIDTH), BF16),
        pltpu.VMEM((2, BPD, BLK, 128), BF16),
        pltpu.VMEM((BPD, 8, 128), BF16),
        pltpu.VMEM((16, WIDTH), BF16),
        pltpu.VMEM((2, 8, 128), BF16),
        pltpu.VMEM((NC, 16, 128), BF16),
        pltpu.VMEM((NC, 8, 128), BF16),
        pltpu.VMEM((SPAN, WIDTH), BF16),
        pltpu.VMEM((SPAN, STATE), BF16),
        pltpu.VMEM((SPAN, STATE), BF16),
        pltpu.VMEM((3, SPAN, 128), F32),
        pltpu.VMEM((SPAN, SPAN), F32),
        pltpu.VMEM((SPAN, WIDTH), F32),
        pltpu.VMEM((SPAN, WIDTH), F32),
        pltpu.VMEM((4, 40, WIDTH), BF16),
        pltpu.VMEM((NC, 40, 128), BF16),
        pltpu.VMEM((NC, 32, 128), BF16),
        pltpu.VMEM((STATE, WIDTH), BF16),
        pltpu.VMEM((8, 2, 16, WIDTH), F32),
        pltpu.VMEM((2, 128, WIDTH), BF16),
        pltpu.VMEM((2, NCHUNK, 4, 16, CW), BF16),
        pltpu.VMEM((2, NCHUNK, 4, 16, CW), BF16),
        pltpu.VMEM((4, 2, 16, CW), F32),
        pltpu.VMEM((2, NCHUNK, 4, 16, CW), F32),
        pltpu.VMEM((2, NCHUNK, 3, 16, CW), BF16),
        pltpu.VMEM((2, NCHUNK, 3, 16, CW), BF16),
        dma(()),
    ]
    scratch += [dma(()) for _ in range(6)] + [dma(()), dma(())] + [dma((2,)), dma((2,))]
    scratch += [dma(()) for _ in range(6)]
    scratch += [dma(()) for _ in range(4)]
    scratch += [dma((2, NCHUNK)), dma((2, NCHUNK)), dma((2, NCHUNK, 3)), dma((2, NCHUNK, 3)), dma(())]
    call = pl.pallas_call(
        body,
        out_shape=jax.ShapeDtypeStruct((SPAN // 8, OUTW), BF16),
        in_specs=[hbm] * 15,
        out_specs=vmem,
        scratch_shapes=scratch,
        compiler_params=pltpu.CompilerParams(
            collective_id=0, has_side_effects=True, vmem_limit_bytes=60 << 20
        ),
        name="layer",
    )
    return call(
        block_order.reshape(1, count),
        doc_lengths.reshape(1, DOCS),
        skip_gain.reshape(1, HEADS),
        values_in.reshape(BPD, BLK, WIDTH),
        gate_in.reshape(BPD, 2, 2, 2, 8, WIDTH),
        keys_in.reshape(BPD, BLK, STATE),
        queries_in.reshape(BPD, BLK, STATE),
        step_in.T,
        conv_values,
        conv_keys,
        conv_queries,
        decay_log.reshape(1, HEADS),
        step_bias.reshape(1, HEADS),
        norm_gain.reshape(1, WIDTH),
        out_weight,
    )


def solution(mesh):
    in_specs = (
        P("ctx", "tp"),
        P("ctx", "tp"),
        P("ctx", "tp"),
        P("ctx", "tp"),
        P("ctx", "tp"),
        P(),
        P(),
        P(None, "tp"),
        P(None, "tp"),
        P(None, "tp"),
        P("tp"),
        P("tp"),
        P("tp"),
        P("tp"),
        P("tp", None),
    )
    out_specs = P(("ctx", "tp"), None)
    return jax.shard_map(
        on_device, mesh=mesh, in_specs=in_specs, out_specs=out_specs, check_vma=False
    )
```
